256 devices in a mesh: batch: 64 (over z, y, core), proto: 4 (over x).
Axes of the slice: x: 4, y: 4, z: 8, core: 2. Of those that a mesh axis runs over, the one named last changes fastest.
Arguments:
- prototypes: bfloat16 [65536, 256], P('proto'), may hold values from -2 to 2
- teacher_embed: bfloat16 [8192, 256], P('batch'), may hold values from -16 to 16
- student_embed: bfloat16 [8192, 256], P('batch'), may hold values from -16 to 16
Outputs:
- grad_prototypes: float32 [65536, 256], P(('proto', 'batch'))
- grad_student: float32 [8192, 256], P('batch')
The draws below stay inside these ranges and needn't reach their ends.
All inputs are finite; a program needn't handle non-finite values.
Results may differ from the reference program's by a relative error of at most 0.0021.
The reference program's roundings to bfloat16 on the way (of `score_grad`) count: a program that leaves them out, or rounds other values in their place, can miss the bound.
Values may be sent and summed in bfloat16 or wider, within the bound.
A program may use at most 128 MiB of HBM per device.

```python
import math
import jax
import jax.numpy as jnp
from jax import lax

D = 256
PROTOS = 65536
CROPS = 8192


def joint_draw(key):
    keys = jax.random.split(jax.random.fold_in(key, 11), 7)
    narrow = D // 16
    column = jnp.arange(D)
    shrink = 0.05
    factor = jnp.where(column < narrow, shrink, 1.0).astype(jnp.float32)
    protos = jnp.clip(jax.random.normal(keys[0], (PROTOS, D), jnp.float32), -6.0, 6.0) * (factor / math.sqrt(D))[None, :]
    common = jnp.where(column < narrow, jax.random.uniform(keys[6], (D,), jnp.float32, 6.0, 10.0), 0.0)
    teacher = 0.1 * jnp.clip(jax.random.normal(keys[1], (CROPS, D), jnp.float32), -6.0, 6.0)
    student = common[None, :] + 0.6 * jnp.clip(jax.random.normal(keys[2], (CROPS, D), jnp.float32), -6.0, 6.0)
    return (protos, teacher, student)


def draw_prototypes(key, part):
    return joint_draw(key)[0].astype(jnp.bfloat16)


def draw_teacher_embed(key, part):
    return joint_draw(key)[1].astype(jnp.bfloat16)


def draw_student_embed(key, part):
    return joint_draw(key)[2].astype(jnp.bfloat16)


def setup_inputs(seed: int = 0) -> dict:
    key_list = jax.random.split(jax.random.key(seed), 4)
    prototypes = draw_prototypes(jax.random.fold_in(key_list[3], 71), 0)
    teacher_embed = draw_teacher_embed(jax.random.fold_in(key_list[3], 71), 0)
    student_embed = draw_student_embed(jax.random.fold_in(key_list[3], 71), 0)
    return dict(prototypes=prototypes, teacher_embed=teacher_embed, student_embed=student_embed)


teacher_temp = 0.07
student_temp = 0.1


def scores(embed, proto_block, temp):
    return jnp.einsum("rd,kd->rk", embed.astype(jnp.float32), proto_block.astype(jnp.float32)) * (1.0 / temp)


def reference(prototypes, teacher_embed, student_embed):
    block_width = min(2048, PROTOS)
    blocks = prototypes.reshape(PROTOS // block_width, block_width, D)

    def peak_pass(carry, proto_block):
        teacher_top, student_top, student_sum = carry
        teacher_top = jnp.maximum(teacher_top, jnp.max(scores(teacher_embed, proto_block, teacher_temp), axis=1))
        student_part = scores(student_embed, proto_block, student_temp)
        fresh_top = jnp.maximum(student_top, jnp.max(student_part, axis=1))
        student_sum = student_sum * jnp.exp(student_top - fresh_top) + jnp.sum(jnp.exp(student_part - fresh_top[:, None]), axis=1)
        return (teacher_top, fresh_top, student_sum), None

    lowest = jnp.full((CROPS,), -jnp.inf, jnp.float32)
    (teacher_peak, student_peak, student_mass), _ = lax.scan(peak_pass, (lowest, lowest, jnp.zeros((CROPS,), jnp.float32)), blocks)

    def column_pass(running, proto_block):
        weights = jnp.exp(scores(teacher_embed, proto_block, teacher_temp) - teacher_peak[:, None])
        col_scale = 1.0 / jnp.sum(weights, axis=0)
        return running + jnp.sum(weights * col_scale[None, :], axis=1), col_scale

    totals, columns = lax.scan(column_pass, jnp.zeros((CROPS,), jnp.float32), blocks)
    row_scale = 1.0 / totals

    def gradient_pass(running, packed):
        proto_block, col_scale = packed
        weights = jnp.exp(scores(teacher_embed, proto_block, teacher_temp) - teacher_peak[:, None])
        targets = weights * row_scale[:, None] * col_scale[None, :]
        probs = jnp.exp(scores(student_embed, proto_block, student_temp) - student_peak[:, None]) / student_mass[:, None]
        score_grad = ((probs - targets) / student_temp).astype(jnp.bfloat16).astype(jnp.float32)
        block_grad = jnp.einsum("rk,rd->kd", score_grad, student_embed.astype(jnp.float32))
        running = running + jnp.einsum("rk,kd->rd", score_grad, proto_block.astype(jnp.float32))
        return running, block_grad

    grad_student, grad_blocks = lax.scan(gradient_pass, jnp.zeros((CROPS, D), jnp.float32), (blocks, columns))
    return grad_blocks.reshape(PROTOS, D), grad_student
```

```python
import functools

import jax
import jax.numpy as jnp
from jax import lax
from jax.experimental import pallas as pl
from jax.experimental.pallas import tpu as pltpu
from jax.sharding import PartitionSpec as P

Y = 4
C = 2
LOG2E = 1.4426950408889634
TEACHER = LOG2E / 0.07
STUDENT = LOG2E / 0.1
LANES = 128
MESH = pl.DeviceIdType.MESH
NT = (((1,), (1,)), ((), ()))
F32 = jnp.float32
BF16 = jnp.bfloat16


def dot_nt(a, b):
    return lax.dot_general(a, b, NT, preferred_element_type=F32)


def dot(a, b):
    return jnp.dot(a, b, preferred_element_type=F32)


def kernel(
    X, Z, p_hbm, te_ref, se_ref, gp_ref, gs_ref,
    p_v, te_all, se_all, ss, init, pe, sg, pt,
    tmx, tmx_r, pk_all, sst, sst_r, sg_all,
    cs, cs_r, csc, rt, rt_r, rz, rz_r, af, bf,
    gacc, gsx_s, gsx_r, gsz_s, gsz_r, gsf,
    gpc_s, gpc_r, gpy_s, gpy_r,
    p_sem, te_ss, te_rs, se_ss, se_rs,
    tx_ss, tx_rs, tz_ss, tz_rs, sx_ss, sx_rs, sz_ss, sz_rs,
    cs_ss, cs_rs, rx_ss, rx_rs, rz_ss, rz_rs,
    gx_ss, gx_rs, gz_ss, gz_rs, gf_ss, gf_rs,
    pc_ss, pc_rs, py_ss, py_rs,
):
    b = lax.axis_index("batch")
    x = lax.axis_index("proto")
    z = b // (Y * C)
    y = (b // C) % Y
    c = b % C
    NP, D = p_v.shape
    KB = NP // Z
    T = KB // (Y * C)
    R = te_ref.shape[0]
    NC = Z // 2
    NT8 = KB // T

    def dev(x_, z_, y_, c_):
        return {"batch": (z_ * Y + y_) * C + c_, "proto": x_}

    xs = [dev((x + d) % X, z, y, c) for d in range(X)]
    zs = [dev(x, (z + d) % Z, y, c) for d in range(Z)]
    ycs = [(dy, dc) for dc in range(C) for dy in range(Y)]
    yc = [dev(x, z, (y + dy) % Y, (c + dc) % C) for dy, dc in ycs]
    pending = []

    def send(src, dst, ssem, rsem, to):
        copy = pltpu.make_async_remote_copy(
            src_ref=src, dst_ref=dst, send_sem=ssem, recv_sem=rsem, device_id=to, device_id_type=MESH
        )
        copy.start()
        pending.append(copy)

    def arrived(dst, ssem, rsem, to):
        pltpu.make_async_remote_copy(
            src_ref=dst, dst_ref=dst, send_sem=ssem, recv_sem=rsem, device_id=to, device_id_type=MESH
        ).wait_recv()

    barrier = pltpu.get_barrier_semaphore()
    peers = xs[1:] + zs[1:] + yc[1:]
    for peer in peers:
        pl.semaphore_signal(barrier, inc=1, device_id=peer, device_id_type=MESH)

    loads = [
        pltpu.make_async_copy(p_hbm.at[pl.ds(i * KB, KB)], p_v.at[pl.ds(i * KB, KB)], p_sem.at[i])
        for i in range(Z)
    ]
    for load in loads:
        load.start()
    te_all[z] = te_ref[...]
    se_all[z] = se_ref[...]

    own = jnp.concatenate([te_ref[...], se_ref[...]], axis=0)
    step = min(512, KB)
    low = jnp.full((32, R), -jnp.inf, F32)
    tops = (low, low)
    for i in range(Z):
        loads[i].wait()

        def stats(k, carry, i=i):
            tm, sm = carry
            at = pl.multiple_of(i * KB + k * step, step)
            s = dot_nt(p_v[pl.ds(at, step), :], own)
            ts = s[:, :R]
            st = s[:, R:]
            ss[pl.ds(at, step), :] = st
            tm = jnp.maximum(tm, jnp.max(ts.reshape(step // 32, 32, R), axis=0))
            sm = jnp.maximum(sm, jnp.max(st.reshape(step // 32, 32, R), axis=0))
            return tm, sm

        tops = lax.fori_loop(0, KB // step, stats, tops)
        if i == min(2, Z - 1):
            pl.semaphore_wait(barrier, len(peers))
            for d in range(1, Z):
                send(te_ref, te_all.at[z], te_ss.at[d], te_rs.at[d], zs[d])
    tmx[...] = jnp.max(tops[0], axis=0, keepdims=True) * TEACHER
    for d in range(1, X):
        send(tmx, tmx_r.at[d], tx_ss.at[d], tx_rs.at[d], xs[d])

    s_top = jnp.max(tops[1], axis=0, keepdims=True) * STUDENT

    def mass(k, acc):
        at = pl.multiple_of(k * step, step)
        e = jnp.exp2(ss[pl.ds(at, step), :] * STUDENT - s_top)
        return acc + jnp.sum(e.reshape(step // 32, 32, R), axis=0)

    half = NP // step // 2
    acc = lax.fori_loop(0, half, mass, jnp.zeros((32, R), F32))
    peak = tmx[...]
    for d in range(1, X):
        arrived(tmx_r.at[d], tx_ss.at[d], tx_rs.at[d], xs[d])
        peak = jnp.maximum(peak, tmx_r[d])
    pk_all[z] = peak
    for d in range(1, Z):
        send(pk_all.at[z], pk_all.at[z], tz_ss.at[d], tz_rs.at[d], zs[d])
    acc = lax.fori_loop(half, NP // step, mass, acc)
    sst[0] = s_top
    sst[1] = jnp.sum(acc, axis=0, keepdims=True)
    for d in range(1, X):
        send(sst, sst_r.at[d], sx_ss.at[d], sx_rs.at[d], xs[d])
    for d in range(1, Z):
        send(se_ref, se_all.at[z], se_ss.at[d], se_rs.at[d], zs[d])

    def turn(k, _):
        tile = p_v[pl.ds(pl.multiple_of(z * KB + k * T, T), T), :]
        pt[k] = tile.T
        return 0

    lax.fori_loop(0, NT8, turn, 0)

    for d in range(1, X):
        arrived(sst_r.at[d], sx_ss.at[d], sx_rs.at[d], xs[d])
    top = sst[0]
    for d in range(1, X):
        top = jnp.maximum(top, sst_r[d, 0])
    total = sst[1] * jnp.exp2(sst[0] - top)
    for d in range(1, X):
        total = total + sst_r[d, 1] * jnp.exp2(sst_r[d, 0] - top)
    sg_all[z, 0] = top
    sg_all[z, 1] = total
    for d in range(1, Z):
        send(sg_all.at[z], sg_all.at[z], sz_ss.at[d], sz_rs.at[d], zs[d])

    for d in range(1, Z):
        arrived(te_all.at[0], te_ss.at[d], te_rs.at[d], zs[d])
    for d in range(1, Z):
        arrived(pk_all.at[0], tz_ss.at[d], tz_rs.at[d], zs[d])

    def pair(ref, j):
        return jnp.concatenate([ref[2 * j], ref[2 * j + 1]], axis=0)

    def row_pair(ref, j):
        return jnp.concatenate([ref[2 * j], ref[2 * j + 1]], axis=1)

    def teach(k, _):
        at = pl.multiple_of(k * T, T)
        tile = p_v[pl.ds(pl.multiple_of(z * KB + k * T, T), T), :]
        part = None
        for j in range(NC):
            e = jnp.exp2(dot_nt(tile, pair(te_all, j)) * TEACHER - row_pair(pk_all, j))
            init[j, pl.ds(at, T), :] = e
            e = e[:, :R] + e[:, R:]
            part = e if part is None else part + e
        for h in range(T // LANES):
            cs[k * (T // LANES) + h] = jnp.sum(part[h * LANES : (h + 1) * LANES].T, axis=0, keepdims=True)
        return 0

    lax.fori_loop(0, NT8, teach, 0)
    for i in range(1, Y * C):
        send(cs, cs_r.at[i], cs_ss.at[i], cs_rs.at[i], yc[i])
    tot = cs[...]
    for i in range(1, Y * C):
        arrived(cs_r.at[i], cs_ss.at[i], cs_rs.at[i], yc[i])
        tot = tot + cs_r[i]
    csc[...] = 1.0 / tot

    def rows(k, accs):
        at = pl.multiple_of(k * LANES, LANES)
        scale = jnp.broadcast_to(csc[k], (LANES, LANES)).T
        out = []
        for j in range(NC):
            for h in range(2):
                v = init[j, pl.ds(at, LANES), h * R : (h + 1) * R] * scale
                init[j, pl.ds(at, LANES), h * R : (h + 1) * R] = v
                out.append(accs[2 * j + h] + jnp.sum(v.reshape(LANES // 8, 8, R), axis=0))
        return tuple(out)

    accs = lax.fori_loop(0, KB // LANES, rows, tuple(jnp.zeros((8, R), F32) for _ in range(Z)))
    for i in range(Z):
        rt[i] = jnp.sum(accs[i], axis=0, keepdims=True)
    for d in range(1, X):
        send(rt, rt_r.at[d], rx_ss.at[d], rx_rs.at[d], xs[d])

    for d in range(1, Z):
        arrived(se_all.at[0], se_ss.at[d], se_rs.at[d], zs[d])
    for d in range(1, Z):
        arrived(sg_all.at[0], sz_ss.at[d], sz_rs.at[d], zs[d])
    for i in range(Z):
        af[i] = 10.0 / sg_all[i, 1]

    def learn(k, _):
        at = pl.multiple_of(k * T, T)
        tile = p_v[pl.ds(pl.multiple_of(z * KB + k * T, T), T), :]
        for j in range(NC):
            tops_j = jnp.concatenate([sg_all[2 * j, 0], sg_all[2 * j + 1, 0]], axis=1)
            pe[j, pl.ds(at, T), :] = jnp.exp2(dot_nt(tile, pair(se_all, j)) * STUDENT - tops_j)
        return 0

    lax.fori_loop(0, NT8 // 2, learn, 0)
    tot = rt[...]
    for d in range(1, X):
        arrived(rt_r.at[d], rx_ss.at[d], rx_rs.at[d], xs[d])
        tot = tot + rt_r[d]
    rz[...] = tot
    for d in range(1, Z):
        send(rz, rz_r.at[d], rz_ss.at[d], rz_rs.at[d], zs[d])
    lax.fori_loop(NT8 // 2, NT8, learn, 0)
    tot = rz[...]
    for d in range(1, Z):
        arrived(rz_r.at[d], rz_ss.at[d], rz_rs.at[d], zs[d])
        tot = tot + rz_r[d]
    bf[...] = 10.0 / tot

    def finish_x(o):
        j = lax.rem(z // 2 + o, NC)
        tot = gacc[o % 2, x]
        for d in range(1, X):
            arrived(gsx_r.at[o, d], gx_ss.at[o, d], gx_rs.at[o, d], xs[d])
            tot = tot + gsx_r[o, d].astype(F32)
        gsz_s[o, 0] = tot[:, :R]
        gsz_s[o, 1] = tot[:, R:]
        for h in range(2):
            if o == 0:
                if h == 1:
                    continue
                to = 1 - z % 2
            else:
                to = h
            send(
                gsz_s.at[o, to], gsz_r.at[z], gz_ss.at[o, h], gz_rs.at[z], dev(x, 2 * j + to, y, c)
            )

    order = list(range(1, NC)) + [0]
    for n, o in enumerate(order):
        j = lax.rem(z // 2 + o, NC)
        a_j = row_pair(af, j)
        b_j = row_pair(bf, j)

        def grad(k, acc, j=j, a_j=a_j, b_j=b_j):
            at = pl.multiple_of(k * T, T)
            g = (pe[j, pl.ds(at, T), :] * a_j - init[j, pl.ds(at, T), :] * b_j).astype(BF16)
            sg[j, pl.ds(at, T), :] = g
            return acc + dot(pt[k], g)

        acc = lax.fori_loop(0, NT8, grad, jnp.zeros((D, 2 * R), F32))
        for q in range(X):
            gacc[o % 2, q] = acc[q * (D // X) : (q + 1) * (D // X)]
        for d in range(1, X):
            gsx_s[o, d] = gacc[o % 2, lax.rem(x + d, X)].astype(BF16)
            send(gsx_s.at[o, d], gsx_r.at[o, d], gx_ss.at[o, d], gx_rs.at[o, d], xs[d])
        if n > 0:
            finish_x(order[n - 1])

    def proto_tile(y_, c_):
        at = pl.multiple_of((y_ * C + c_) * T, T)
        g = None
        for j in range(NC):
            part = dot(sg[j, pl.ds(at, T), :], pair(se_all, j))
            g = part if g is None else g + part
        return g

    partner = yc[Y]
    for k in range(Y):
        gpc_s[k] = proto_tile(lax.rem(y + 1 + k, Y), 1 - c)
        send(gpc_s.at[k], gpc_r.at[k], pc_ss.at[k], pc_rs.at[k], partner)
        if k == 0:
            finish_x(order[-1])
    keep = None
    for k in range(Y):
        g = proto_tile(lax.rem(y + 1 + k, Y), c)
        arrived(gpc_r.at[k], pc_ss.at[k], pc_rs.at[k], partner)
        g = g + gpc_r[k]
        if k < Y - 1:
            gpy_s[k] = g.astype(BF16)
            send(gpy_s.at[k], gpy_r.at[k], py_ss.at[k], py_rs.at[k], yc[k + 1])
        else:
            gp_ref[...] = g

    tot = gsz_s[0, z % 2]
    for d in range(1, Z):
        src = lax.rem(z + d, Z)
        arrived(gsz_r.at[src], gz_ss.at[0, 0], gz_rs.at[src], zs[d])
        tot = tot + gsz_r[src]
    gsf[x] = tot
    for d in range(1, X):
        send(gsf.at[x], gsf.at[x], gf_ss.at[d], gf_rs.at[d], xs[d])
    for k in range(Y - 1):
        arrived(gpy_r.at[k], py_ss.at[k], py_rs.at[k], yc[k + 1])
        gp_ref[...] += gpy_r[k].astype(F32)
    for d in range(1, X):
        arrived(gsf.at[0], gf_ss.at[d], gf_rs.at[d], xs[d])
    full = gsf[...].reshape(D, R)
    for h in range(D // LANES):
        gs_ref[:, h * LANES : (h + 1) * LANES] = full[h * LANES : (h + 1) * LANES].T
    for copy in pending:
        copy.wait_send()


def local(X, Z, prototypes, teacher_embed, student_embed):
    NP, D = prototypes.shape
    R = teacher_embed.shape[0]
    KB = NP // Z
    T = KB // (Y * C)
    NC = Z // 2
    NT8 = Y * C
    Q = D // X
    V = pltpu.VMEM
    dma = pltpu.SemaphoreType.DMA
    vmem = pl.BlockSpec(memory_space=pltpu.VMEM)
    scratch = [
        V((NP, D), BF16), V((Z, R, D), BF16), V((Z, R, D), BF16), V((NP, R), F32),
        V((NC, KB, 2 * R), F32), V((NC, KB, 2 * R), F32), V((NC, KB, 2 * R), BF16), V((NT8, D, T), BF16),
        V((1, R), F32), V((X, 1, R), F32), V((Z, 1, R), F32),
        V((2, 1, R), F32), V((X, 2, 1, R), F32), V((Z, 2, 1, R), F32),
        V((KB // LANES, 1, LANES), F32), V((Y * C, KB // LANES, 1, LANES), F32), V((KB // LANES, 1, LANES), F32),
        V((Z, 1, R), F32), V((X, Z, 1, R), F32), V((Z, 1, R), F32), V((Z, Z, 1, R), F32),
        V((Z, 1, R), F32), V((Z, 1, R), F32),
        V((2, X, Q, 2 * R), F32), V((NC, X, Q, 2 * R), BF16), V((NC, X, Q, 2 * R), BF16),
        V((NC, 2, Q, R), F32), V((Z, Q, R), F32), V((X, Q, R), F32),
        V((Y, T, D), F32), V((Y, T, D), F32), V((Y, T, D), BF16), V((Y, T, D), BF16),
        dma((Z,)), dma((Z,)), dma((Z,)), dma((Z,)), dma((Z,)),
        dma((X,)), dma((X,)), dma((Z,)), dma((Z,)), dma((X,)), dma((X,)), dma((Z,)), dma((Z,)),
        dma((Y * C,)), dma((Y * C,)), dma((X,)), dma((X,)), dma((Z,)), dma((Z,)),
        dma((NC, X)), dma((NC, X)), dma((NC, 2)), dma((Z,)), dma((X,)), dma((X,)),
        dma((Y,)), dma((Y,)), dma((Y,)), dma((Y,)),
    ]
    return pl.pallas_call(
        functools.partial(kernel, X, Z),
        out_shape=(jax.ShapeDtypeStruct((T, D), F32), jax.ShapeDtypeStruct((R, D), F32)),
        in_specs=[pl.BlockSpec(memory_space=pl.ANY), vmem, vmem],
        out_specs=(vmem, vmem),
        scratch_shapes=scratch,
        compiler_params=pltpu.CompilerParams(
            collective_id=0, has_side_effects=True, vmem_limit_bytes=60 << 20
        ),
        name="head",
    )(prototypes, teacher_embed, student_embed)


def solution(mesh):
    X = mesh.shape["proto"]
    Z = mesh.shape["batch"] // (Y * C)
    placed = (P("proto", None), P("batch", None), P("batch", None))
    return jax.shard_map(
        functools.partial(local, X, Z),
        mesh=mesh,
        in_specs=placed,
        out_specs=(P(("proto", "batch"), None), P("batch", None)),
        check_vma=False,
    )
```

```python
import functools
import math

import jax
import jax.numpy as jnp
from jax import lax
from jax.experimental import pallas as pl
from jax.experimental.pallas import tpu as pltpu
from jax.sharding import PartitionSpec as P

Y = 4
C = 2
LOG2E = 1.4426950408889634
TEACHER = LOG2E / 0.07
STUDENT = LOG2E / 0.1
LANES = 128
MESH = pl.DeviceIdType.MESH
NT = (((1,), (1,)), ((), ()))
F32 = jnp.float32
BF16 = jnp.bfloat16
GROUPS = 5


def dot_nt(a, b):
    return lax.dot_general(a, b, NT, preferred_element_type=F32)


def dot(a, b):
    return jnp.dot(a, b, preferred_element_type=F32)


def kernel(
    X, Z, p_hbm, te_hbm, se_hbm, out_hbm,
    p_v, te_all, se_all, ss, init, pe, sg, pt,
    tmx, tmx_r, pk_all, sst, sst_r, sg_all,
    csp, cs, cs_r, csc, rt, rt_r, rz, rz_r, af, bf,
    gacc, hx_s, hx_r, gsx_s, gsx_r, gsz_s, gsz_r, gsf,
    gpc_s, gpc_r, hy_s, hy_r, gy, gpy_s, gpy_r, gs_v,
    p_sem, o_sem, out_sem, te_rs, se_rs, tx_rs, tz_rs, sx_rs, sz_rs, cs_rs, rx_rs, rz_rs,
    hx_rs, gx_rs, gz_rs, gf_rs, pc_rs, hy_rs, py_rs,
):
    b = lax.axis_index("batch")
    x = lax.axis_index("proto")
    z = b // (Y * C)
    y = (b // C) % Y
    c = b % C
    NP, D = p_v.shape
    KB = NP // Z
    T = KB // (Y * C)
    R = te_all.shape[1]
    NC = Z // 2
    NT8 = KB // T

    def dev(x_, z_, y_, c_):
        return {"batch": (z_ * Y + y_) * C + c_, "proto": x_}

    xs = [dev((x + d) % X, z, y, c) for d in range(X)]
    zs = [dev(x, (z + d) % Z, y, c) for d in range(Z)]
    ycs = [(dy, dc) for dc in range(C) for dy in range(Y)]
    yc = [dev(x, z, (y + dy) % Y, (c + dc) % C) for dy, dc in ycs]
    sent = [0] * GROUPS

    def send(src, dst, rsem, to, group):
        pltpu.make_async_remote_copy(
            src_ref=src, dst_ref=dst, send_sem=out_sem.at[group], recv_sem=rsem, device_id=to, device_id_type=MESH
        ).start()
        sent[group] += math.prod(src.shape) * src.dtype.itemsize

    def arrived(dst, rsem):
        pltpu.make_async_remote_copy(
            src_ref=dst, dst_ref=dst, send_sem=out_sem.at[0], recv_sem=rsem, device_id=xs[1], device_id_type=MESH
        ).wait_recv()

    own_t = pltpu.make_async_copy(te_hbm, te_all.at[z], o_sem.at[0])
    own_s = pltpu.make_async_copy(se_hbm, se_all.at[z], o_sem.at[1])
    own_t.start()
    own_s.start()

    def load(i):
        at = pl.multiple_of(i * KB, KB)
        return pltpu.make_async_copy(p_hbm.at[pl.ds(at, KB)], p_v.at[pl.ds(at, KB)], p_sem.at[i])

    ahead = min(3, Z)
    for i in range(ahead):
        load(i).start()
    barrier = pltpu.get_barrier_semaphore()
    peers = xs[1:] + zs[1:] + yc[1:]
    for peer in peers:
        pl.semaphore_signal(barrier, inc=1, device_id=peer, device_id_type=MESH)
    own_t.wait()
    own_s.wait()

    HR = R // 2

    def gather_near(full, rs, group):
        if Z != 8:
            for d in range(1, Z):
                send(full.at[z], full.at[z], rs.at[2], zs[d], group)
            return
        for d in (2, 6, 1, 7):
            slot = {2: 0, 6: 1}.get(d, 2)
            send(full.at[z], full.at[z], rs.at[slot], zs[d], group)

    def gather_far(full, rs, group):
        if Z != 8:
            return
        below = lax.rem(z + 6, 8)
        above = lax.rem(z + 2, 8)
        arrived(full.at[below], rs.at[0])
        send(full.at[below, :HR], full.at[below, :HR], rs.at[2], zs[2], group)
        send(full.at[below], full.at[below], rs.at[2], zs[1], group)
        arrived(full.at[above], rs.at[1])
        send(full.at[above, HR:], full.at[above, HR:], rs.at[2], zs[6], group)
        send(full.at[above], full.at[above], rs.at[2], zs[7], group)

    def gather_end(full, rs):
        arrived(full.at[pl.ds(0, 5 if Z == 8 else Z - 1)], rs.at[2])

    own = jnp.concatenate([te_all[z], se_all[z]], axis=0)
    low = jnp.full((32, R), -jnp.inf, F32)

    def stats(i, carry):
        tm, sm = carry
        load(i).wait()

        @pl.when(i + ahead < Z)
        def _():
            load(i + ahead).start()

        at = pl.multiple_of(i * KB, KB)
        s = dot_nt(p_v[pl.ds(at, KB), :], own)
        ts = s[:, :R]
        st = s[:, R:]
        ss[pl.ds(at, KB), :] = st
        tm = jnp.maximum(tm, jnp.max(ts.reshape(KB // 32, 32, R), axis=0))
        sm = jnp.maximum(sm, jnp.max(st.reshape(KB // 32, 32, R), axis=0))
        return tm, sm

    early = min(3, Z)
    tops = lax.fori_loop(0, early, stats, (low, low))
    pl.semaphore_wait(barrier, len(peers))
    gather_near(te_all, te_rs, 0)
    tops = lax.fori_loop(early, Z, stats, tops)
    tmx[...] = jnp.max(tops[0], axis=0, keepdims=True) * TEACHER
    for d in range(1, X):
        send(tmx, tmx_r.at[d], tx_rs.at[0], xs[d], 4)

    s_top = jnp.max(tops[1], axis=0, keepdims=True) * STUDENT
    step = min(512, KB)

    def mass(k, acc):
        at = pl.multiple_of(k * step, step)
        e = jnp.exp2(ss[pl.ds(at, step), :] * STUDENT - s_top)
        return acc + jnp.sum(e.reshape(step // 32, 32, R), axis=0)

    half = NP // step // 2
    acc = lax.fori_loop(0, half, mass, jnp.zeros((32, R), F32))
    peak = tmx[...]
    arrived(tmx_r.at[pl.ds(1, X - 1)], tx_rs.at[0])
    for d in range(1, X):
        peak = jnp.maximum(peak, tmx_r[d])
    pk_all[z] = peak
    for d in range(1, Z):
        send(pk_all.at[z], pk_all.at[z], tz_rs.at[0], zs[d], 4)
    gather_far(te_all, te_rs, 0)
    gather_near(se_all, se_rs, 1)
    acc = lax.fori_loop(half, NP // step, mass, acc)
    sst[0] = s_top
    sst[1] = jnp.sum(acc, axis=0, keepdims=True)
    for d in range(1, X):
        send(sst, sst_r.at[d], sx_rs.at[0], xs[d], 4)
    for k in range(NT8):
        tile = p_v[pl.ds(pl.multiple_of(z * KB + k * T, T), T), :]
        pt[:, k * T : (k + 1) * T] = tile.T
    arrived(pk_all.at[pl.ds(0, Z - 1)], tz_rs.at[0])
    gather_end(te_all, te_rs)

    def pair(ref, j):
        return jnp.concatenate([ref[2 * j], ref[2 * j + 1]], axis=0)

    def row_pair(ref, j):
        return jnp.concatenate([ref[2 * j], ref[2 * j + 1]], axis=1)

    block = p_v.at[pl.ds(pl.multiple_of(z * KB, KB), KB)]
    for j in range(NC):
        e = jnp.exp2(dot_nt(block[...], pair(te_all, j)) * TEACHER - row_pair(pk_all, j))
        init[j] = e
        e = e[:, :R] + e[:, R:]
        csp[...] = e if j == 0 else csp[...] + e
    for h in range(KB // LANES):
        cs[h] = jnp.sum(csp[h * LANES : (h + 1) * LANES].T, axis=0, keepdims=True)
    for i in range(1, Y * C):
        send(cs, cs_r.at[i], cs_rs.at[0], yc[i], 0)
    arrived(sst_r.at[pl.ds(1, X - 1)], sx_rs.at[0])
    top = sst[0]
    for d in range(1, X):
        top = jnp.maximum(top, sst_r[d, 0])
    total = sst[1] * jnp.exp2(sst[0] - top)
    for d in range(1, X):
        total = total + sst_r[d, 1] * jnp.exp2(sst_r[d, 0] - top)
    sg_all[z, 0] = top
    sg_all[z, 1] = total
    for d in range(1, Z):
        send(sg_all.at[z], sg_all.at[z], sz_rs.at[0], zs[d], 4)
    gather_far(se_all, se_rs, 1)
    tot = cs[...]
    arrived(cs_r.at[pl.ds(1, Y * C - 1)], cs_rs.at[0])
    for i in range(1, Y * C):
        tot = tot + cs_r[i]
    csc[...] = 1.0 / tot

    def rows(k, accs):
        at = pl.multiple_of(k * LANES, LANES)
        scale = jnp.broadcast_to(csc[k], (LANES, LANES)).T
        out = []
        for j in range(NC):
            for h in range(2):
                v = init[j, pl.ds(at, LANES), h * R : (h + 1) * R] * scale
                init[j, pl.ds(at, LANES), h * R : (h + 1) * R] = v
                out.append(accs[2 * j + h] + jnp.sum(v.reshape(LANES // 8, 8, R), axis=0))
        return tuple(out)

    accs = lax.fori_loop(0, KB // LANES, rows, tuple(jnp.zeros((8, R), F32) for _ in range(Z)), unroll=4)
    for i in range(Z):
        rt[i] = jnp.sum(accs[i], axis=0, keepdims=True)
    for d in range(1, X):
        send(rt, rt_r.at[d], rx_rs.at[0], xs[d], 0)
    gather_end(se_all, se_rs)
    arrived(sg_all.at[pl.ds(0, Z - 1)], sz_rs.at[0])
    for i in range(Z):
        af[i] = 10.0 / sg_all[i, 1]

    def learn(j):
        tops_j = jnp.concatenate([sg_all[2 * j, 0], sg_all[2 * j + 1, 0]], axis=1)
        pe[j] = jnp.exp2(dot_nt(block[...], pair(se_all, j)) * STUDENT - tops_j)

    for j in range(NC // 2):
        learn(j)
    tot = rt[...]
    arrived(rt_r.at[pl.ds(1, X - 1)], rx_rs.at[0])
    for d in range(1, X):
        tot = tot + rt_r[d]
    rz[...] = tot
    for d in range(1, Z):
        send(rz, rz_r.at[d], rz_rs.at[0], zs[d], 0)
    for j in range(NC // 2, NC):
        learn(j)
    tot = rz[...]
    arrived(rz_r.at[pl.ds(1, Z - 1)], rz_rs.at[0])
    for d in range(1, Z):
        tot = tot + rz_r[d]
    bf[...] = 10.0 / tot

    Q = D // X
    HQ = Q // 2
    HT = T // 2
    order = list(range(1, NC)) + [0]

    def piece(o, d):
        return gacc.at[o, lax.rem(x + d, X)]

    def to_x(o, side, part, value):
        gsx_s[o, side, part] = value.astype(BF16)
        send(gsx_s.at[o, side, part], gsx_r.at[o, side, part], gx_rs.at[o], xs[1 if side == 0 else 3], 2)

    def x_first(o):
        for side in range(2):
            hx_s[o, side] = piece(o, 2)[side * HQ : (side + 1) * HQ].astype(BF16)
            send(hx_s.at[o, side], hx_r.at[o, side], hx_rs.at[o], xs[1 if side == 0 else 3], 2)
        to_x(o, 0, 1, piece(o, 1)[HQ:])
        to_x(o, 1, 0, piece(o, 3)[:HQ])

    def x_second(o):
        arrived(hx_r.at[o], hx_rs.at[o])
        to_x(o, 0, 0, piece(o, 1)[:HQ] + hx_r[o, 0].astype(F32))
        to_x(o, 1, 1, piece(o, 3)[HQ:] + hx_r[o, 1].astype(F32))

    def x_third(o):
        j = lax.rem(z // 2 + o, NC)
        arrived(gsx_r.at[o], gx_rs.at[o])
        for part in range(2):
            tot = piece(o, 0)[part * HQ : (part + 1) * HQ]
            for side in range(2):
                tot = tot + gsx_r[o, side, part].astype(F32)
            gsz_s[o, 0, part * HQ : (part + 1) * HQ] = tot[:, :R]
            gsz_s[o, 1, part * HQ : (part + 1) * HQ] = tot[:, R:]
        if o == 0:
            to = 1 - z % 2
            send(gsz_s.at[o, to], gsz_r.at[z], gz_rs.at[0], dev(x, 2 * j + to, y, c), 2)
        else:
            for h in range(2):
                send(gsz_s.at[o, h], gsz_r.at[z], gz_rs.at[0], dev(x, 2 * j + h, y, c), 2)

    for n, o in enumerate(order):
        j = lax.rem(z // 2 + o, NC)
        g = (pe[j] * row_pair(af, j) - init[j] * row_pair(bf, j)).astype(BF16)
        sg[j] = g
        acc = dot(pt[...], g)
        for q in range(X):
            gacc[o, q] = acc[q * Q : (q + 1) * Q]
        x_first(o)
        if n == 3:
            x_second(order[0])

    def proto_tiles(deltas, c_):
        lhs = []
        for d in deltas:
            at = pl.multiple_of((lax.rem(y + d, Y) * C + c_) * T, T)
            lhs.append(jnp.concatenate([sg[j, pl.ds(at, T), :] for j in range(NC)], axis=1))
        return dot(jnp.concatenate(lhs, axis=0), se_all[...].reshape(Z * R, D))

    partner = yc[Y]

    def to_partner(n, deltas):
        g = proto_tiles(deltas, 1 - c)
        for i in range(2):
            gpc_s[n, i] = g[i * T : (i + 1) * T]
        send(gpc_s.at[n], gpc_r.at[n], pc_rs.at[n], partner, 3)

    def to_y(side, part, value):
        gpy_s[side, part] = value.astype(BF16)
        send(gpy_s.at[side, part], gpy_r.at[side, part], py_rs.at[0], yc[1 if side == 0 else 3], 3)

    seconds = order[1:] if NC > 3 else order
    to_partner(0, (2, 1))
    for o in seconds[:1]:
        x_second(o)
    to_partner(1, (3, 0))
    for o in seconds[1:]:
        x_second(o)
    g = proto_tiles((2, 1), c)
    arrived(gpc_r.at[0], pc_rs.at[0])
    for side in range(2):
        at = side * HT
        hy_s[side] = (g[at : at + HT] + gpc_r[0, 0, at : at + HT]).astype(BF16)
        send(hy_s.at[side], hy_r.at[side], hy_rs.at[0], yc[1 if side == 0 else 3], 3)
    to_y(0, 1, g[T + HT :] + gpc_r[0, 1, HT:])
    gy[0] = g[T : T + HT] + gpc_r[0, 1, :HT]
    for o in order[:2]:
        x_third(o)
    g = proto_tiles((3, 0), c)
    arrived(gpc_r.at[1], pc_rs.at[1])
    to_y(1, 0, g[:HT] + gpc_r[1, 0, :HT])
    gy[1] = g[HT:T] + gpc_r[1, 0, HT:]
    gy[2] = g[T : T + HT] + gpc_r[1, 1, :HT]
    gy[3] = g[T + HT :] + gpc_r[1, 1, HT:]
    for o in order[2:]:
        x_third(o)
    arrived(hy_r, hy_rs.at[0])
    to_y(0, 0, gy[0] + hy_r[0].astype(F32))
    to_y(1, 1, gy[1] + hy_r[1].astype(F32))
    arrived(gsz_r.at[pl.ds(0, Z - 1)], gz_rs.at[0])
    tot = gsz_s[0, z % 2]
    for d in range(1, Z):
        tot = tot + gsz_r[lax.rem(z + d, Z)]
    gsf[x] = tot
    for d in range(1, X):
        send(gsf.at[x], gsf.at[x], gf_rs.at[0], xs[d], 3)
    arrived(gpy_r, py_rs.at[0])
    for part in range(2):
        tot = gy[2 + part]
        for side in range(2):
            tot = tot + gpy_r[side, part].astype(F32)
        gy[2 + part] = tot
    outs = [
        pltpu.make_async_copy(gy.at[2 + part], out_hbm.at[pl.ds(part * HT, HT)], o_sem.at[part])
        for part in range(2)
    ]
    for out in outs:
        out.start()
    arrived(gsf.at[pl.ds(0, X - 1)], gf_rs.at[0])
    full = gsf[...].reshape(D, R)
    for h in range(D // LANES):
        gs_v[:, h * LANES : (h + 1) * LANES] = full[h * LANES : (h + 1) * LANES].T
    out = pltpu.make_async_copy(gs_v, out_hbm.at[pl.ds(T, R)], o_sem.at[2])
    out.start()
    outs.append(out)
    for group, size in enumerate(sent):
        n = size // (2 * D)
        whole = cs_r.at[pl.ds(0, 2), pl.ds(0, n // 2)] if group == 4 else p_v.at[pl.ds(0, n)]
        pltpu.make_async_remote_copy(
            src_ref=whole, dst_ref=whole, send_sem=out_sem.at[group],
            recv_sem=tx_rs.at[0], device_id=xs[1], device_id_type=MESH,
        ).wait_send()
    for out in outs:
        out.wait()


def local(X, Z, prototypes, teacher_embed, student_embed):
    NP, D = prototypes.shape
    R = teacher_embed.shape[0]
    KB = NP // Z
    T = KB // (Y * C)
    NC = Z // 2
    Q = D // X
    HQ = Q // 2
    HT = T // 2
    V = pltpu.VMEM
    dma = pltpu.SemaphoreType.DMA
    hbm = pl.BlockSpec(memory_space=pl.ANY)
    scratch = [
        V((NP, D), BF16), V((Z, R, D), BF16), V((Z, R, D), BF16), V((NP, R), F32),
        V((NC, KB, 2 * R), F32), V((NC, KB, 2 * R), F32), V((NC, KB, 2 * R), BF16), V((D, KB), BF16),
        V((1, R), F32), V((X, 1, R), F32), V((Z, 1, R), F32),
        V((2, 1, R), F32), V((X, 2, 1, R), F32), V((Z, 2, 1, R), F32),
        V((KB, R), F32), V((KB // LANES, 1, LANES), F32), V((Y * C, KB // LANES, 1, LANES), F32),
        V((KB // LANES, 1, LANES), F32),
        V((Z, 1, R), F32), V((X, Z, 1, R), F32), V((Z, 1, R), F32), V((Z, Z, 1, R), F32),
        V((Z, 1, R), F32), V((Z, 1, R), F32),
        V((NC, X, Q, 2 * R), F32), V((NC, 2, HQ, 2 * R), BF16), V((NC, 2, HQ, 2 * R), BF16),
        V((NC, 2, 2, HQ, 2 * R), BF16), V((NC, 2, 2, HQ, 2 * R), BF16),
        V((NC, 2, Q, R), F32), V((Z, Q, R), F32), V((X, Q, R), F32),
        V((2, 2, T, D), F32), V((2, 2, T, D), F32), V((2, HT, D), BF16), V((2, HT, D), BF16), V((4, HT, D), F32),
        V((2, 2, HT, D), BF16), V((2, 2, HT, D), BF16), V((R, D), F32),
        dma((Z,)), dma((3,)), dma((GROUPS,)), dma((3,)), dma((3,)), *[dma((1,))] * 7,
        dma((NC,)), dma((NC,)), dma((1,)), dma((1,)), dma((2,)), dma((1,)), dma((1,)),
    ]
    out = pl.pallas_call(
        functools.partial(kernel, X, Z),
        out_shape=jax.ShapeDtypeStruct((T + R, D), F32),
        in_specs=[hbm, hbm, hbm],
        out_specs=hbm,
        scratch_shapes=scratch,
        compiler_params=pltpu.CompilerParams(
            collective_id=0, has_side_effects=True, vmem_limit_bytes=63 << 20
        ),
        name="head",
    )(prototypes, teacher_embed, student_embed)
    return out[:T], out[T:]


def solution(mesh):
    X = mesh.shape["proto"]
    Z = mesh.shape["batch"] // (Y * C)
    placed = (P("proto", None), P("batch", None), P("batch", None))
    return jax.shard_map(
        functools.partial(local, X, Z),
        mesh=mesh,
        in_specs=placed,
        out_specs=(P(("proto", "batch"), None), P("batch", None)),
        check_vma=False,
    )
```

```python
import functools
import math

import jax
import jax.numpy as jnp
from jax import lax
from jax.experimental import pallas as pl
from jax.experimental.pallas import tpu as pltpu
from jax.sharding import PartitionSpec as P

Y = 4
C = 2
LOG2E = 1.4426950408889634
TEACHER = LOG2E / 0.07
STUDENT = LOG2E / 0.1
LANES = 128
MESH = pl.DeviceIdType.MESH
NT = (((1,), (1,)), ((), ()))
F32 = jnp.float32
BF16 = jnp.bfloat16
GROUPS = 5
NARROW = (2,)


def dot_nt(a, b):
    return lax.dot_general(a, b, NT, preferred_element_type=F32)


def dot(a, b):
    return jnp.dot(a, b, preferred_element_type=F32)


def kernel(
    X, Z, p_hbm, te_hbm, se_hbm, out_hbm,
    p_v, te_all, se_all, ss, init, pe, sg, pt,
    tmx, tmx_r, pk_all, sst, sst_r, sg_all,
    csp, cs, cs_r, csc, rt, rt_r, rz, rz_r, af, bf,
    gacc, hx_s, hx_r, gsx_s, gsx_r, gxs_s, gxs_r, gsz_s, gsz_r, gszb_s, gszb_r, gsf,
    gpc_s, gpc_r, hy_s, hy_r, gy, gpy_s, gpy_r, gs_v,
    p_sem, o_sem, out_sem, te_rs, se_rs, tx_rs, tz_rs, sx_rs, sz_rs, cs_rs, rx_rs, rz_rs,
    hx_rs, gx_rs, gxs_rs, gz_rs, gzb_rs, gf_rs, pc_rs, hy_rs, py_rs,
):
    b = lax.axis_index("batch")
    x = lax.axis_index("proto")
    z = b // (Y * C)
    y = (b // C) % Y
    c = b % C
    NP, D = p_v.shape
    KB = NP // Z
    T = KB // (Y * C)
    R = te_all.shape[1]
    NC = Z // 2
    NT8 = KB // T

    def dev(x_, z_, y_, c_):
        return {"batch": (z_ * Y + y_) * C + c_, "proto": x_}

    xs = [dev((x + d) % X, z, y, c) for d in range(X)]
    zs = [dev(x, (z + d) % Z, y, c) for d in range(Z)]
    ycs = [(dy, dc) for dc in range(C) for dy in range(Y)]
    yc = [dev(x, z, (y + dy) % Y, (c + dc) % C) for dy, dc in ycs]
    sent = [0] * GROUPS

    def send(src, dst, rsem, to, group):
        pltpu.make_async_remote_copy(
            src_ref=src, dst_ref=dst, send_sem=out_sem.at[group], recv_sem=rsem, device_id=to, device_id_type=MESH
        ).start()
        sent[group] += math.prod(src.shape) * src.dtype.itemsize

    def arrived(dst, rsem):
        pltpu.make_async_remote_copy(
            src_ref=dst, dst_ref=dst, send_sem=out_sem.at[0], recv_sem=rsem, device_id=xs[1], device_id_type=MESH
        ).wait_recv()

    own_t = pltpu.make_async_copy(te_hbm, te_all.at[z], o_sem.at[0])
    own_s = pltpu.make_async_copy(se_hbm, se_all.at[z], o_sem.at[1])
    own_t.start()
    own_s.start()

    def load(i):
        at = pl.multiple_of(i * KB, KB)
        return pltpu.make_async_copy(p_hbm.at[pl.ds(at, KB)], p_v.at[pl.ds(at, KB)], p_sem.at[i])

    ahead = min(3, Z)
    for i in range(ahead):
        load(i).start()
    barrier = pltpu.get_barrier_semaphore()
    peers = xs[1:] + zs[1:] + yc[1:]
    for peer in peers:
        pl.semaphore_signal(barrier, inc=1, device_id=peer, device_id_type=MESH)
    own_t.wait()
    own_s.wait()

    HR = R // 2

    def gather_near(full, rs, group):
        if Z != 8:
            for d in range(1, Z):
                send(full.at[z], full.at[z], rs.at[2], zs[d], group)
            return
        for d in (2, 6, 1, 7):
            slot = {2: 0, 6: 1}.get(d, 2)
            send(full.at[z], full.at[z], rs.at[slot], zs[d], group)

    def gather_far(full, rs, group):
        if Z != 8:
            return
        below = lax.rem(z + 6, 8)
        above = lax.rem(z + 2, 8)
        arrived(full.at[below], rs.at[0])
        send(full.at[below, :HR], full.at[below, :HR], rs.at[2], zs[2], group)
        send(full.at[below], full.at[below], rs.at[2], zs[1], group)
        arrived(full.at[above], rs.at[1])
        send(full.at[above, HR:], full.at[above, HR:], rs.at[2], zs[6], group)
        send(full.at[above], full.at[above], rs.at[2], zs[7], group)

    def gather_end(full, rs):
        arrived(full.at[pl.ds(0, 5 if Z == 8 else Z - 1)], rs.at[2])

    own = jnp.concatenate([te_all[z], se_all[z]], axis=0)
    low = jnp.full((32, R), -jnp.inf, F32)

    def stats(i, carry):
        tm, sm = carry
        load(i).wait()

        @pl.when(i + ahead < Z)
        def _():
            load(i + ahead).start()

        at = pl.multiple_of(i * KB, KB)
        s = dot_nt(p_v[pl.ds(at, KB), :], own)
        ts = s[:, :R]
        st = s[:, R:]
        ss[pl.ds(at, KB), :] = st
        tm = jnp.maximum(tm, jnp.max(ts.reshape(KB // 32, 32, R), axis=0))
        sm = jnp.maximum(sm, jnp.max(st.reshape(KB // 32, 32, R), axis=0))
        return tm, sm

    early = min(3, Z)
    tops = lax.fori_loop(0, early, stats, (low, low))
    pl.semaphore_wait(barrier, len(peers))
    gather_near(te_all, te_rs, 0)
    tops = lax.fori_loop(early, Z, stats, tops)
    tmx[...] = jnp.max(tops[0], axis=0, keepdims=True) * TEACHER
    for d in range(1, X):
        send(tmx, tmx_r.at[d], tx_rs.at[0], xs[d], 4)

    s_top = jnp.max(tops[1], axis=0, keepdims=True) * STUDENT
    step = min(512, KB)

    def mass(k, acc):
        at = pl.multiple_of(k * step, step)
        e = jnp.exp2(ss[pl.ds(at, step), :] * STUDENT - s_top)
        return acc + jnp.sum(e.reshape(step // 32, 32, R), axis=0)

    half = NP // step // 2
    acc = lax.fori_loop(0, half, mass, jnp.zeros((32, R), F32))
    peak = tmx[...]
    arrived(tmx_r.at[pl.ds(1, X - 1)], tx_rs.at[0])
    for d in range(1, X):
        peak = jnp.maximum(peak, tmx_r[d])
    pk_all[z] = peak
    for d in range(1, Z):
        send(pk_all.at[z], pk_all.at[z], tz_rs.at[0], zs[d], 4)
    gather_far(te_all, te_rs, 0)
    acc = lax.fori_loop(half, NP // step, mass, acc)
    sst[0] = s_top
    sst[1] = jnp.sum(acc, axis=0, keepdims=True)
    for d in range(1, X):
        send(sst, sst_r.at[d], sx_rs.at[0], xs[d], 4)
    for k in range(NT8):
        tile = p_v[pl.ds(pl.multiple_of(z * KB + k * T, T), T), :]
        pt[:, k * T : (k + 1) * T] = tile.T
    arrived(pk_all.at[pl.ds(0, Z - 1)], tz_rs.at[0])
    gather_end(te_all, te_rs)
    gather_near(se_all, se_rs, 1)

    def pair(ref, j):
        return jnp.concatenate([ref[2 * j], ref[2 * j + 1]], axis=0)

    def row_pair(ref, j):
        return jnp.concatenate([ref[2 * j], ref[2 * j + 1]], axis=1)

    block = p_v.at[pl.ds(pl.multiple_of(z * KB, KB), KB)]
    for j in range(NC):
        e = jnp.exp2(dot_nt(block[...], pair(te_all, j)) * TEACHER - row_pair(pk_all, j))
        init[j] = e
        e = e[:, :R] + e[:, R:]
        csp[...] = e if j == 0 else csp[...] + e
    for h in range(KB // LANES):
        cs[h] = jnp.sum(csp[h * LANES : (h + 1) * LANES].T, axis=0, keepdims=True)
    for i in range(1, Y * C):
        send(cs, cs_r.at[i], cs_rs.at[0], yc[i], 0)
    arrived(sst_r.at[pl.ds(1, X - 1)], sx_rs.at[0])
    top = sst[0]
    for d in range(1, X):
        top = jnp.maximum(top, sst_r[d, 0])
    total = sst[1] * jnp.exp2(sst[0] - top)
    for d in range(1, X):
        total = total + sst_r[d, 1] * jnp.exp2(sst_r[d, 0] - top)
    sg_all[z, 0] = top
    sg_all[z, 1] = total
    for d in range(1, Z):
        send(sg_all.at[z], sg_all.at[z], sz_rs.at[0], zs[d], 4)
    gather_far(se_all, se_rs, 1)
    tot = cs[...]
    arrived(cs_r.at[pl.ds(1, Y * C - 1)], cs_rs.at[0])
    for i in range(1, Y * C):
        tot = tot + cs_r[i]
    csc[...] = 1.0 / tot

    def rows(k, accs):
        at = pl.multiple_of(k * LANES, LANES)
        scale = jnp.broadcast_to(csc[k], (LANES, LANES)).T
        out = []
        for j in range(NC):
            for h in range(2):
                v = init[j, pl.ds(at, LANES), h * R : (h + 1) * R] * scale
                init[j, pl.ds(at, LANES), h * R : (h + 1) * R] = v
                out.append(accs[2 * j + h] + jnp.sum(v.reshape(LANES // 8, 8, R), axis=0))
        return tuple(out)

    accs = lax.fori_loop(0, KB // LANES, rows, tuple(jnp.zeros((8, R), F32) for _ in range(Z)), unroll=4)
    for i in range(Z):
        rt[i] = jnp.sum(accs[i], axis=0, keepdims=True)
    for d in range(1, X):
        send(rt, rt_r.at[d], rx_rs.at[0], xs[d], 0)

    def learn(j):
        tops_j = jnp.concatenate([sg_all[2 * j, 0], sg_all[2 * j + 1, 0]], axis=1)
        pe[j] = jnp.exp2(dot_nt(block[...], pair(se_all, j)) * STUDENT - tops_j)

    tot = rt[...]
    arrived(rt_r.at[pl.ds(1, X - 1)], rx_rs.at[0])
    for d in range(1, X):
        tot = tot + rt_r[d]
    rz[...] = tot
    for d in range(1, Z):
        send(rz, rz_r.at[d], rz_rs.at[0], zs[d], 0)
    gather_end(se_all, se_rs)
    arrived(sg_all.at[pl.ds(0, Z - 1)], sz_rs.at[0])
    for i in range(Z):
        af[i] = 10.0 / sg_all[i, 1]
    for j in range(NC):
        learn(j)
    tot = rz[...]
    arrived(rz_r.at[pl.ds(1, Z - 1)], rz_rs.at[0])
    for d in range(1, Z):
        tot = tot + rz_r[d]
    bf[...] = 10.0 / tot

    Q = D // X
    HQ = Q // 2
    HT = T // 2
    narrow = NARROW if NC == 4 else ()
    order = [2, 1, 3, 0] if NC == 4 else list(range(1, NC)) + [0]

    def piece(o, d):
        return gacc.at[o, lax.rem(x + d, X)]

    def x_first(o):
        for side in range(2):
            to = xs[1 if side == 0 else 3]
            hx_s[o, side] = piece(o, 2)[side * HQ : (side + 1) * HQ].astype(BF16)
            send(hx_s.at[o, side], hx_r.at[o, side], hx_rs.at[o], to, 2)
            at = (1 - side) * HQ
            gsx_s[o, side] = piece(o, 1 if side == 0 else 3)[at : at + HQ].astype(BF16)
            send(gsx_s.at[o, side], gsx_r.at[o, side], gx_rs.at[o], to, 2)

    def x_second(o):
        arrived(hx_r.at[o], hx_rs.at[o])
        for side in range(2):
            at = side * HQ
            gxs_s[o, side] = piece(o, 1 if side == 0 else 3)[at : at + HQ] + hx_r[o, side].astype(F32)
            send(gxs_s.at[o, side], gxs_r.at[o, side], gxs_rs.at[o], xs[1 if side == 0 else 3], 2)

    def x_third(o):
        j = lax.rem(z // 2 + o, NC)
        arrived(gsx_r.at[o], gx_rs.at[o])
        arrived(gxs_r.at[o], gxs_rs.at[o])
        keep, there, rsem = (gszb_s, gszb_r, gzb_rs) if o in narrow else (gsz_s, gsz_r, gz_rs)
        for part in range(2):
            at = part * HQ
            tot = piece(o, 0)[at : at + HQ] + gxs_r[o, part] + gsx_r[o, 1 - part].astype(F32)
            for h in range(2):
                keep[o, h, at : at + HQ] = tot[:, h * R : (h + 1) * R].astype(keep.dtype)
        for h in range(1 if o == 0 else 2):
            to = 1 - z % 2 if o == 0 else h
            send(keep.at[o, to], there.at[z], rsem.at[0], dev(x, 2 * j + to, y, c), 2)

    for n, o in enumerate(order):
        j = lax.rem(z // 2 + o, NC)
        g = (pe[j] * row_pair(af, j) - init[j] * row_pair(bf, j)).astype(BF16)
        sg[j] = g
        acc = dot(pt[...], g)
        for q in range(X):
            gacc[o, q] = acc[q * Q : (q + 1) * Q]
        x_first(o)

    def proto_tiles(deltas, c_):
        lhs = []
        for d in deltas:
            at = pl.multiple_of((lax.rem(y + d, Y) * C + c_) * T, T)
            lhs.append(jnp.concatenate([sg[j, pl.ds(at, T), :] for j in range(NC)], axis=1))
        return dot(jnp.concatenate(lhs, axis=0), se_all[...].reshape(Z * R, D))

    partner = yc[Y]

    def to_partner(n, deltas):
        g = proto_tiles(deltas, 1 - c)
        for i in range(len(deltas)):
            gpc_s[n + i] = g[i * T : (i + 1) * T]
        send(gpc_s.at[pl.ds(n, len(deltas))], gpc_r.at[pl.ds(n, len(deltas))], pc_rs.at[n], partner, 3)

    def to_y(side, part, value):
        gpy_s[side, part] = value.astype(BF16)
        send(gpy_s.at[side, part], gpy_r.at[side, part], py_rs.at[0], yc[1 if side == 0 else 3], 3)

    steps = [("s", o) for o in order] + [("t", o) for o in order]

    def advance(count):
        for _ in range(min(count, len(steps))):
            kind, o = steps.pop(0)
            (x_second if kind == "s" else x_third)(o)

    to_partner(0, (2,))
    advance(1)
    to_partner(1, (1, 3))
    advance(1)
    g = proto_tiles((2,), c)
    advance(1)
    arrived(gpc_r.at[pl.ds(0, 1)], pc_rs.at[0])
    for side in range(2):
        at = side * HT
        hy_s[side] = (g[at : at + HT] + gpc_r[0, at : at + HT]).astype(BF16)
        send(hy_s.at[side], hy_r.at[side], hy_rs.at[0], yc[1 if side == 0 else 3], 3)
    advance(2)
    to_partner(3, (0,))
    advance(1)
    g = proto_tiles((1, 3), c)
    advance(1)
    arrived(gpc_r.at[pl.ds(1, 2)], pc_rs.at[1])
    to_y(0, 1, g[HT:T] + gpc_r[1, HT:])
    gy[0] = g[:HT] + gpc_r[1, :HT]
    to_y(1, 0, g[T : T + HT] + gpc_r[2, :HT])
    gy[1] = g[T + HT :] + gpc_r[2, HT:]
    advance(len(steps))
    g = proto_tiles((0,), c)
    gy[2] = g[:HT]
    gy[3] = g[HT:]
    arrived(hy_r, hy_rs.at[0])
    to_y(0, 0, gy[0] + hy_r[0].astype(F32))
    to_y(1, 1, gy[1] + hy_r[1].astype(F32))
    arrived(gsz_r.at[pl.ds(0, Z - 1 - 2 * len(narrow))], gz_rs.at[0])
    if narrow:
        arrived(gszb_r.at[pl.ds(0, 2 * len(narrow))], gzb_rs.at[0])
    tot = gsz_s[0, z % 2]
    tot = tot + gsz_r[z + 1 - 2 * (z % 2)]
    for o in range(1, NC):
        j = lax.rem(z // 2 + o, NC)
        for h in range(2):
            tot = tot + (gszb_r if NC - o in narrow else gsz_r)[2 * j + h].astype(F32)
    gsf[x] = tot
    for d in range(1, X):
        send(gsf.at[x], gsf.at[x], gf_rs.at[0], xs[d], 3)
    arrived(gpy_r, py_rs.at[0])
    arrived(gpc_r.at[pl.ds(3, 1)], pc_rs.at[3])
    for part in range(2):
        tot = gy[2 + part] + gpc_r[3, part * HT : (part + 1) * HT]
        for side in range(2):
            tot = tot + gpy_r[side, part].astype(F32)
        gy[2 + part] = tot
    outs = [
        pltpu.make_async_copy(gy.at[2 + part], out_hbm.at[pl.ds(part * HT, HT)], o_sem.at[part])
        for part in range(2)
    ]
    for out in outs:
        out.start()
    arrived(gsf.at[pl.ds(0, X - 1)], gf_rs.at[0])
    full = gsf[...].reshape(D, R)
    for h in range(D // LANES):
        gs_v[:, h * LANES : (h + 1) * LANES] = full[h * LANES : (h + 1) * LANES].T
    out = pltpu.make_async_copy(gs_v, out_hbm.at[pl.ds(T, R)], o_sem.at[2])
    out.start()
    outs.append(out)
    for group, size in enumerate(sent):
        n = size // (2 * D)
        whole = cs_r.at[pl.ds(0, 2), pl.ds(0, n // 2)] if group == 4 else p_v.at[pl.ds(0, n)]
        pltpu.make_async_remote_copy(
            src_ref=whole, dst_ref=whole, send_sem=out_sem.at[group],
            recv_sem=tx_rs.at[0], device_id=xs[1], device_id_type=MESH,
        ).wait_send()
    for out in outs:
        out.wait()


def split(in_hbm, gp_hbm, gs_hbm, buf, i_sem, o_sem):
    T = gp_hbm.shape[0]
    R = gs_hbm.shape[0]
    ins = [
        pltpu.make_async_copy(in_hbm.at[pl.ds(at, n)], buf.at[pl.ds(at, n)], i_sem.at[k])
        for k, (at, n) in enumerate(((0, T), (T, R)))
    ]
    outs = [
        pltpu.make_async_copy(buf.at[pl.ds(0, T)], gp_hbm, o_sem.at[0]),
        pltpu.make_async_copy(buf.at[pl.ds(T, R)], gs_hbm, o_sem.at[1]),
    ]
    for copy in ins:
        copy.start()
    for copy, out in zip(ins, outs):
        copy.wait()
        out.start()
    for out in outs:
        out.wait()


def local(X, Z, prototypes, teacher_embed, student_embed):
    NP, D = prototypes.shape
    R = teacher_embed.shape[0]
    KB = NP // Z
    T = KB // (Y * C)
    NC = Z // 2
    Q = D // X
    HQ = Q // 2
    HT = T // 2
    V = pltpu.VMEM
    dma = pltpu.SemaphoreType.DMA
    hbm = pl.BlockSpec(memory_space=pl.ANY)
    scratch = [
        V((NP, D), BF16), V((Z, R, D), BF16), V((Z, R, D), BF16), V((NP, R), F32),
        V((NC, KB, 2 * R), F32), V((NC, KB, 2 * R), F32), V((NC, KB, 2 * R), BF16), V((D, KB), BF16),
        V((1, R), F32), V((X, 1, R), F32), V((Z, 1, R), F32),
        V((2, 1, R), F32), V((X, 2, 1, R), F32), V((Z, 2, 1, R), F32),
        V((KB, R), F32), V((KB // LANES, 1, LANES), F32), V((Y * C, KB // LANES, 1, LANES), F32),
        V((KB // LANES, 1, LANES), F32),
        V((Z, 1, R), F32), V((X, Z, 1, R), F32), V((Z, 1, R), F32), V((Z, Z, 1, R), F32),
        V((Z, 1, R), F32), V((Z, 1, R), F32),
        V((NC, X, Q, 2 * R), F32), V((NC, 2, HQ, 2 * R), BF16), V((NC, 2, HQ, 2 * R), BF16),
        V((NC, 2, HQ, 2 * R), BF16), V((NC, 2, HQ, 2 * R), BF16), V((NC, 2, HQ, 2 * R), F32), V((NC, 2, HQ, 2 * R), F32),
        V((NC, 2, Q, R), F32), V((Z, Q, R), F32), V((NC, 2, Q, R), BF16), V((Z, Q, R), BF16), V((X, Q, R), F32),
        V((Y, T, D), F32), V((Y, T, D), F32), V((2, HT, D), BF16), V((2, HT, D), BF16), V((4, HT, D), F32),
        V((2, 2, HT, D), BF16), V((2, 2, HT, D), BF16), V((R, D), F32),
        dma((Z,)), dma((3,)), dma((GROUPS,)), dma((3,)), dma((3,)), *[dma((1,))] * 7,
        dma((NC,)), dma((NC,)), dma((NC,)), dma((1,)), dma((1,)), dma((1,)), dma((Y,)), dma((1,)), dma((1,)),
    ]
    out = pl.pallas_call(
        functools.partial(kernel, X, Z),
        out_shape=jax.ShapeDtypeStruct((T + R, D), F32),
        in_specs=[hbm, hbm, hbm],
        out_specs=hbm,
        scratch_shapes=scratch,
        compiler_params=pltpu.CompilerParams(
            collective_id=0, has_side_effects=True, vmem_limit_bytes=63 << 20
        ),
        name="head",
    )(prototypes, teacher_embed, student_embed)
    return pl.pallas_call(
        split,
        out_shape=(jax.ShapeDtypeStruct((T, D), F32), jax.ShapeDtypeStruct((R, D), F32)),
        in_specs=[hbm],
        out_specs=(hbm, hbm),
        scratch_shapes=[V((T + R, D), F32), dma((2,)), dma((2,))],
        name="split",
    )(out)


def solution(mesh):
    X = mesh.shape["proto"]
    Z = mesh.shape["batch"] // (Y * C)
    placed = (P("proto", None), P("batch", None), P("batch", None))
    return jax.shard_map(
        functools.partial(local, X, Z),
        mesh=mesh,
        in_specs=placed,
        out_specs=(P(("proto", "batch"), None), P("batch", None)),
        check_vma=False,
    )
```

```python
import functools
import math

import jax
import jax.numpy as jnp
from jax import lax
from jax.experimental import pallas as pl
from jax.experimental.pallas import tpu as pltpu
from jax.sharding import PartitionSpec as P

Y = 4
C = 2
LOG2E = 1.4426950408889634
TEACHER = LOG2E / 0.07
STUDENT = LOG2E / 0.1
LANES = 128
MESH = pl.DeviceIdType.MESH
NT = (((1,), (1,)), ((), ()))
F32 = jnp.float32
BF16 = jnp.bfloat16
GROUPS = 5
NARROW = (1, 2)


def dot_nt(a, b):
    return lax.dot_general(a, b, NT, preferred_element_type=F32)


def dot(a, b):
    return jnp.dot(a, b, preferred_element_type=F32)


def kernel(
    X, Z, p_hbm, te_hbm, se_hbm, out_hbm,
    p_v, te_all, se_all, ss, init, pe, sg, pt,
    tmx, tmx_r, pk_all, sst, sst_r, sg_all,
    csp, cs, cs_r, csc, rt, rt_r, rz, rz_r, af, bf,
    gacc, hx_s, hx_r, gsx_s, gsx_r, gxs_s, gxs_r, gsz_s, gsz_r, gszb_s, gszb_r, gsf,
    gpc_s, gpc_r, hy_s, hy_r, gy, gpy_s, gpy_r, gs_v,
    p_sem, o_sem, out_sem, te_rs, se_rs, tx_rs, tz_rs, sx_rs, sz_rs, cs_rs, rx_rs, rz_rs,
    hx_rs, gx_rs, gxs_rs, gz_rs, gzb_rs, gf_rs, pc_rs, hy_rs, py_rs,
):
    b = lax.axis_index("batch")
    x = lax.axis_index("proto")
    z = b // (Y * C)
    y = (b // C) % Y
    c = b % C
    NP, D = p_v.shape
    KB = NP // Z
    T = KB // (Y * C)
    R = te_all.shape[1]
    NC = Z // 2
    NT8 = KB // T

    def dev(x_, z_, y_, c_):
        return {"batch": (z_ * Y + y_) * C + c_, "proto": x_}

    xs = [dev((x + d) % X, z, y, c) for d in range(X)]
    zs = [dev(x, (z + d) % Z, y, c) for d in range(Z)]
    ycs = [(dy, dc) for dc in range(C) for dy in range(Y)]
    yc = [dev(x, z, (y + dy) % Y, (c + dc) % C) for dy, dc in ycs]
    sent = [0] * GROUPS

    def send(src, dst, rsem, to, group):
        pltpu.make_async_remote_copy(
            src_ref=src, dst_ref=dst, send_sem=out_sem.at[group], recv_sem=rsem, device_id=to, device_id_type=MESH
        ).start()
        sent[group] += math.prod(src.shape) * src.dtype.itemsize

    def arrived(dst, rsem):
        pltpu.make_async_remote_copy(
            src_ref=dst, dst_ref=dst, send_sem=out_sem.at[0], recv_sem=rsem, device_id=xs[1], device_id_type=MESH
        ).wait_recv()

    own_t = pltpu.make_async_copy(te_hbm, te_all.at[z], o_sem.at[0])
    own_s = pltpu.make_async_copy(se_hbm, se_all.at[z], o_sem.at[1])
    own_t.start()
    own_s.start()

    def load(i):
        at = pl.multiple_of(i * KB, KB)
        return pltpu.make_async_copy(p_hbm.at[pl.ds(at, KB)], p_v.at[pl.ds(at, KB)], p_sem.at[i])

    ahead = min(4, Z)
    for i in range(2):
        load(i).start()
    barrier = pltpu.get_barrier_semaphore()
    peers = xs[1:] + zs[1:] + yc[1:]
    for peer in peers:
        pl.semaphore_signal(barrier, inc=1, device_id=peer, device_id_type=MESH)
    own_t.wait()
    own_s.wait()
    for i in range(2, ahead):
        load(i).start()

    HR = R // 2

    def gather_near(full, rs, group):
        if Z != 8:
            for d in range(1, Z):
                send(full.at[z], full.at[z], rs.at[4], zs[d], group)
            return
        for part in range(2):
            for d in (2, 6):
                low_half = (part == 0) == (d == 2)
                rows = pl.ds(0 if low_half else HR, HR)
                send(full.at[z, rows], full.at[z, rows], rs.at[part + (0 if d == 2 else 2)], zs[d], group)
        for d in (1, 7):
            send(full.at[z], full.at[z], rs.at[4], zs[d], group)

    def gather_far(full, rs, group):
        if Z != 8:
            return
        for part in range(2):
            for d in (2, 6):
                src = lax.rem(z + 8 - d, 8)
                low_half = (part == 0) == (d == 2)
                rows = pl.ds(0 if low_half else HR, HR)
                arrived(full.at[src, rows], rs.at[part + (0 if d == 2 else 2)])
                if part == 0:
                    send(full.at[src, rows], full.at[src, rows], rs.at[4], zs[d], group)
                send(full.at[src, rows], full.at[src, rows], rs.at[4], zs[1 if d == 2 else 7], group)

    def gather_end(full, rs):
        arrived(full.at[pl.ds(0, 5 if Z == 8 else Z - 1)], rs.at[4])

    own = jnp.concatenate([te_all[z], se_all[z]], axis=0)
    low = jnp.full((32, R), -jnp.inf, F32)

    def stats(i, carry, n=1):
        tm, sm = carry
        for k in range(n):
            load(i + k).wait()
        for k in range(n):

            @pl.when(i + k + ahead < Z)
            def _():
                load(i + k + ahead).start()

        at = pl.multiple_of(i * KB, KB)
        s = dot_nt(p_v[pl.ds(at, n * KB), :], own)
        ts = s[:, :R]
        st = s[:, R:]
        ss[pl.ds(at, n * KB), :] = st
        tm = jnp.maximum(tm, jnp.max(ts.reshape(n * KB // 32, 32, R), axis=0))
        sm = jnp.maximum(sm, jnp.max(st.reshape(n * KB // 32, 32, R), axis=0))
        return tm, sm

    def stats_pair(k, tops):
        return stats(2 * k, tops, 2)

    early = min(2, NC)
    tops = lax.fori_loop(0, early, stats_pair, (low, low))
    pl.semaphore_wait(barrier, len(peers))
    gather_near(te_all, te_rs, 0)
    tops = lax.fori_loop(early, NC, stats_pair, tops)
    tmx[...] = jnp.max(tops[0], axis=0, keepdims=True) * TEACHER
    for d in range(1, X):
        send(tmx, tmx_r.at[d], tx_rs.at[0], xs[d], 4)

    s_top = jnp.max(tops[1], axis=0, keepdims=True) * STUDENT
    step = min(512, KB)

    def mass(k, acc):
        at = pl.multiple_of(k * step, step)
        e = jnp.exp2(ss[pl.ds(at, step), :] * STUDENT - s_top)
        return acc + jnp.sum(e.reshape(step // 32, 32, R), axis=0)

    half = NP // step // 2
    acc = lax.fori_loop(0, half, mass, jnp.zeros((32, R), F32))
    peak = tmx[...]
    arrived(tmx_r.at[pl.ds(1, X - 1)], tx_rs.at[0])
    for d in range(1, X):
        peak = jnp.maximum(peak, tmx_r[d])
    pk_all[z] = peak
    for d in range(1, Z):
        send(pk_all.at[z], pk_all.at[z], tz_rs.at[0], zs[d], 4)
    gather_far(te_all, te_rs, 0)
    acc = lax.fori_loop(half, NP // step, mass, acc)
    sst[0] = s_top
    sst[1] = jnp.sum(acc, axis=0, keepdims=True)
    for d in range(1, X):
        send(sst, sst_r.at[d], sx_rs.at[0], xs[d], 4)
    for k in range(NT8):
        tile = p_v[pl.ds(pl.multiple_of(z * KB + k * T, T), T), :]
        pt[:, k * T : (k + 1) * T] = tile.T
    arrived(pk_all.at[pl.ds(0, Z - 1)], tz_rs.at[0])
    gather_end(te_all, te_rs)
    gather_near(se_all, se_rs, 1)

    def pair(ref, j):
        return jnp.concatenate([ref[2 * j], ref[2 * j + 1]], axis=0)

    def row_pair(ref, j):
        return jnp.concatenate([ref[2 * j], ref[2 * j + 1]], axis=1)

    block = p_v.at[pl.ds(pl.multiple_of(z * KB, KB), KB)]
    for j in range(NC):
        e = jnp.exp2(dot_nt(block[...], pair(te_all, j)) * TEACHER - row_pair(pk_all, j))
        init[j] = e
        e = e[:, :R] + e[:, R:]
        csp[...] = e if j == 0 else csp[...] + e
    for h in range(KB // LANES):
        cs[h] = jnp.sum(csp[h * LANES : (h + 1) * LANES].T, axis=0, keepdims=True)
    for i in range(1, Y * C):
        send(cs, cs_r.at[i], cs_rs.at[0], yc[i], 0)
    arrived(sst_r.at[pl.ds(1, X - 1)], sx_rs.at[0])
    top = sst[0]
    for d in range(1, X):
        top = jnp.maximum(top, sst_r[d, 0])
    total = sst[1] * jnp.exp2(sst[0] - top)
    for d in range(1, X):
        total = total + sst_r[d, 1] * jnp.exp2(sst_r[d, 0] - top)
    sg_all[z, 0] = top
    sg_all[z, 1] = total
    for d in range(1, Z):
        send(sg_all.at[z], sg_all.at[z], sz_rs.at[0], zs[d], 4)
    gather_far(se_all, se_rs, 1)
    tot = cs[...]
    arrived(cs_r.at[pl.ds(1, Y * C - 1)], cs_rs.at[0])
    for i in range(1, Y * C):
        tot = tot + cs_r[i]
    csc[...] = 1.0 / tot

    def rows(k, accs):
        at = pl.multiple_of(k * LANES, LANES)
        scale = jnp.broadcast_to(csc[k], (LANES, LANES)).T
        out = []
        for j in range(NC):
            for h in range(2):
                v = init[j, pl.ds(at, LANES), h * R : (h + 1) * R] * scale
                init[j, pl.ds(at, LANES), h * R : (h + 1) * R] = v
                out.append(accs[2 * j + h] + jnp.sum(v.reshape(LANES // 8, 8, R), axis=0))
        return tuple(out)

    accs = lax.fori_loop(0, KB // LANES, rows, tuple(jnp.zeros((8, R), F32) for _ in range(Z)), unroll=8)
    for i in range(Z):
        rt[i] = jnp.sum(accs[i], axis=0, keepdims=True)
    for d in range(1, X):
        send(rt, rt_r.at[d], rx_rs.at[0], xs[d], 0)

    def learn(j):
        tops_j = jnp.concatenate([sg_all[2 * j, 0], sg_all[2 * j + 1, 0]], axis=1)
        pe[j] = jnp.exp2(dot_nt(block[...], pair(se_all, j)) * STUDENT - tops_j)

    tot = rt[...]
    arrived(rt_r.at[pl.ds(1, X - 1)], rx_rs.at[0])
    for d in range(1, X):
        tot = tot + rt_r[d]
    rz[...] = tot
    for d in range(1, Z):
        send(rz, rz_r.at[d], rz_rs.at[0], zs[d], 0)
    gather_end(se_all, se_rs)
    arrived(sg_all.at[pl.ds(0, Z - 1)], sz_rs.at[0])
    for i in range(Z):
        af[i] = 10.0 / sg_all[i, 1]
    for j in range(NC):
        learn(j)
    tot = rz[...]
    arrived(rz_r.at[pl.ds(1, Z - 1)], rz_rs.at[0])
    for d in range(1, Z):
        tot = tot + rz_r[d]
    bf[...] = 10.0 / tot

    Q = D // X
    HQ = Q // 2
    HT = T // 2
    narrow = NARROW if NC == 4 else ()
    order = [2, 1, 3, 0] if NC == 4 else list(range(1, NC)) + [0]

    def piece(o, d):
        return gacc.at[o, lax.rem(x + d, X)]

    def x_first(o):
        for side in range(2):
            to = xs[1 if side == 0 else 3]
            hx_s[o, side] = piece(o, 2)[side * HQ : (side + 1) * HQ].astype(BF16)
            send(hx_s.at[o, side], hx_r.at[o, side], hx_rs.at[o], to, 2)
            at = (1 - side) * HQ
            gsx_s[o, side] = piece(o, 1 if side == 0 else 3)[at : at + HQ].astype(BF16)
            send(gsx_s.at[o, side], gsx_r.at[o, side], gx_rs.at[o], to, 2)

    def x_second(o):
        arrived(hx_r.at[o], hx_rs.at[o])
        for side in range(2):
            at = side * HQ
            gxs_s[o, side] = piece(o, 1 if side == 0 else 3)[at : at + HQ] + hx_r[o, side].astype(F32)
            send(gxs_s.at[o, side], gxs_r.at[o, side], gxs_rs.at[o], xs[1 if side == 0 else 3], 2)

    def x_third(o):
        j = lax.rem(z // 2 + o, NC)
        arrived(gsx_r.at[o], gx_rs.at[o])
        arrived(gxs_r.at[o], gxs_rs.at[o])
        keep, there, rsem = (gszb_s, gszb_r, gzb_rs) if o in narrow else (gsz_s, gsz_r, gz_rs)
        for part in range(2):
            at = part * HQ
            tot = piece(o, 0)[at : at + HQ] + gxs_r[o, part] + gsx_r[o, 1 - part].astype(F32)
            for h in range(2):
                keep[o, h, at : at + HQ] = tot[:, h * R : (h + 1) * R].astype(keep.dtype)
        for h in range(1 if o == 0 else 2):
            to = 1 - z % 2 if o == 0 else h
            send(keep.at[o, to], there.at[z], rsem.at[0], dev(x, 2 * j + to, y, c), 2)

    for n in range(0, NC, 2):
        group = order[n : n + 2]
        gs = []
        for o in group:
            j = lax.rem(z // 2 + o, NC)
            g = (pe[j] * row_pair(af, j) - init[j] * row_pair(bf, j)).astype(BF16)
            sg[j] = g
            gs.append(g)
        acc = dot(pt[...], jnp.concatenate(gs, axis=1))
        for i, o in enumerate(group):
            for q in range(X):
                gacc[o, q] = acc[q * Q : (q + 1) * Q, i * 2 * R : (i + 1) * 2 * R]
            x_first(o)

    def proto_tiles(deltas, c_):
        lhs = []
        for d in deltas:
            at = pl.multiple_of((lax.rem(y + d, Y) * C + c_) * T, T)
            lhs.append(jnp.concatenate([sg[j, pl.ds(at, T), :] for j in range(NC)], axis=1))
        return dot(jnp.concatenate(lhs, axis=0), se_all[...].reshape(Z * R, D))

    partner = yc[Y]

    def to_partner(n, deltas):
        g = proto_tiles(deltas, 1 - c)
        for i in range(len(deltas)):
            gpc_s[n + i] = g[i * T : (i + 1) * T]
        send(gpc_s.at[pl.ds(n, len(deltas))], gpc_r.at[pl.ds(n, len(deltas))], pc_rs.at[n], partner, 3)

    def to_y(side, part, value):
        gpy_s[side, part] = value.astype(BF16)
        send(gpy_s.at[side, part], gpy_r.at[side, part], py_rs.at[0], yc[1 if side == 0 else 3], 3)

    steps = [("s", o) for o in order] + [("t", o) for o in order]

    def advance(count):
        for _ in range(min(count, len(steps))):
            kind, o = steps.pop(0)
            (x_second if kind == "s" else x_third)(o)

    to_partner(0, (2,))
    to_partner(1, (1, 3))
    advance(1)
    g = proto_tiles((2,), c)
    advance(3)
    arrived(gpc_r.at[pl.ds(0, 1)], pc_rs.at[0])
    for side in range(2):
        at = side * HT
        hy_s[side] = (g[at : at + HT] + gpc_r[0, at : at + HT]).astype(BF16)
        send(hy_s.at[side], hy_r.at[side], hy_rs.at[0], yc[1 if side == 0 else 3], 3)
    to_partner(3, (0,))
    advance(2)
    g = proto_tiles((1, 3), c)
    advance(1)
    arrived(gpc_r.at[pl.ds(1, 2)], pc_rs.at[1])
    to_y(0, 1, g[HT:T] + gpc_r[1, HT:])
    gy[0] = g[:HT] + gpc_r[1, :HT]
    to_y(1, 0, g[T : T + HT] + gpc_r[2, :HT])
    gy[1] = g[T + HT :] + gpc_r[2, HT:]
    advance(len(steps))
    g = proto_tiles((0,), c)
    gy[2] = g[:HT]
    gy[3] = g[HT:]
    arrived(hy_r, hy_rs.at[0])
    to_y(0, 0, gy[0] + hy_r[0].astype(F32))
    to_y(1, 1, gy[1] + hy_r[1].astype(F32))
    arrived(gsz_r.at[pl.ds(0, Z - 1 - 2 * len(narrow))], gz_rs.at[0])
    if narrow:
        arrived(gszb_r.at[pl.ds(0, 2 * len(narrow))], gzb_rs.at[0])
    tot = gsz_s[0, z % 2]
    tot = tot + gsz_r[z + 1 - 2 * (z % 2)]
    for o in range(1, NC):
        j = lax.rem(z // 2 + o, NC)
        for h in range(2):
            tot = tot + (gszb_r if NC - o in narrow else gsz_r)[2 * j + h].astype(F32)
    gsf[x] = tot
    for d in range(1, X):
        send(gsf.at[x], gsf.at[x], gf_rs.at[0], xs[d], 3)
    arrived(gpy_r, py_rs.at[0])
    arrived(gpc_r.at[pl.ds(3, 1)], pc_rs.at[3])
    for part in range(2):
        tot = gy[2 + part] + gpc_r[3, part * HT : (part + 1) * HT]
        for side in range(2):
            tot = tot + gpy_r[side, part].astype(F32)
        gy[2 + part] = tot
    outs = [
        pltpu.make_async_copy(gy.at[2 + part], out_hbm.at[pl.ds(part * HT, HT)], o_sem.at[part])
        for part in range(2)
    ]
    for out in outs:
        out.start()
    arrived(gsf.at[pl.ds(0, X - 1)], gf_rs.at[0])
    full = gsf[...].reshape(D, R)
    for h in range(D // LANES):
        gs_v[:, h * LANES : (h + 1) * LANES] = full[h * LANES : (h + 1) * LANES].T
    out = pltpu.make_async_copy(gs_v, out_hbm.at[pl.ds(T, R)], o_sem.at[2])
    out.start()
    outs.append(out)
    for group, size in enumerate(sent):
        n = size // (2 * D)
        whole = cs_r.at[pl.ds(0, 2), pl.ds(0, n // 2)] if group == 4 else p_v.at[pl.ds(0, n)]
        pltpu.make_async_remote_copy(
            src_ref=whole, dst_ref=whole, send_sem=out_sem.at[group],
            recv_sem=tx_rs.at[0], device_id=xs[1], device_id_type=MESH,
        ).wait_send()
    for out in outs:
        out.wait()


def split(in_hbm, gp_hbm, gs_hbm, buf, i_sem, o_sem):
    T = gp_hbm.shape[0]
    R = gs_hbm.shape[0]
    ins = [
        pltpu.make_async_copy(in_hbm.at[pl.ds(at, n)], buf.at[pl.ds(at, n)], i_sem.at[k])
        for k, (at, n) in enumerate(((0, T), (T, R)))
    ]
    outs = [
        pltpu.make_async_copy(buf.at[pl.ds(0, T)], gp_hbm, o_sem.at[0]),
        pltpu.make_async_copy(buf.at[pl.ds(T, R)], gs_hbm, o_sem.at[1]),
    ]
    for copy in ins:
        copy.start()
    for copy, out in zip(ins, outs):
        copy.wait()
        out.start()
    for out in outs:
        out.wait()


def local(X, Z, prototypes, teacher_embed, student_embed):
    NP, D = prototypes.shape
    R = teacher_embed.shape[0]
    KB = NP // Z
    T = KB // (Y * C)
    NC = Z // 2
    Q = D // X
    HQ = Q // 2
    HT = T // 2
    V = pltpu.VMEM
    dma = pltpu.SemaphoreType.DMA
    hbm = pl.BlockSpec(memory_space=pl.ANY)
    scratch = [
        V((NP, D), BF16), V((Z, R, D), BF16), V((Z, R, D), BF16), V((NP, R), F32),
        V((NC, KB, 2 * R), F32), V((NC, KB, 2 * R), F32), V((NC, KB, 2 * R), BF16), V((D, KB), BF16),
        V((1, R), F32), V((X, 1, R), F32), V((Z, 1, R), F32),
        V((2, 1, R), F32), V((X, 2, 1, R), F32), V((Z, 2, 1, R), F32),
        V((KB, R), F32), V((KB // LANES, 1, LANES), F32), V((Y * C, KB // LANES, 1, LANES), F32),
        V((KB // LANES, 1, LANES), F32),
        V((Z, 1, R), F32), V((X, Z, 1, R), F32), V((Z, 1, R), F32), V((Z, Z, 1, R), F32),
        V((Z, 1, R), F32), V((Z, 1, R), F32),
        V((NC, X, Q, 2 * R), F32), V((NC, 2, HQ, 2 * R), BF16), V((NC, 2, HQ, 2 * R), BF16),
        V((NC, 2, HQ, 2 * R), BF16), V((NC, 2, HQ, 2 * R), BF16), V((NC, 2, HQ, 2 * R), F32), V((NC, 2, HQ, 2 * R), F32),
        V((NC, 2, Q, R), F32), V((Z, Q, R), F32), V((NC, 2, Q, R), BF16), V((Z, Q, R), BF16), V((X, Q, R), F32),
        V((Y, T, D), F32), V((Y, T, D), F32), V((2, HT, D), BF16), V((2, HT, D), BF16), V((4, HT, D), F32),
        V((2, 2, HT, D), BF16), V((2, 2, HT, D), BF16), V((R, D), F32),
        dma((Z,)), dma((3,)), dma((GROUPS,)), dma((5,)), dma((5,)), *[dma((1,))] * 7,
        dma((NC,)), dma((NC,)), dma((NC,)), dma((1,)), dma((1,)), dma((1,)), dma((Y,)), dma((1,)), dma((1,)),
    ]
    out = pl.pallas_call(
        functools.partial(kernel, X, Z),
        out_shape=jax.ShapeDtypeStruct((T + R, D), F32),
        in_specs=[hbm, hbm, hbm],
        out_specs=hbm,
        scratch_shapes=scratch,
        compiler_params=pltpu.CompilerParams(
            collective_id=0, has_side_effects=True, vmem_limit_bytes=63 << 20
        ),
        name="head",
    )(prototypes, teacher_embed, student_embed)
    return pl.pallas_call(
        split,
        out_shape=(jax.ShapeDtypeStruct((T, D), F32), jax.ShapeDtypeStruct((R, D), F32)),
        in_specs=[hbm],
        out_specs=(hbm, hbm),
        scratch_shapes=[V((T + R, D), F32), dma((2,)), dma((2,))],
        name="split",
    )(out)


def solution(mesh):
    X = mesh.shape["proto"]
    Z = mesh.shape["batch"] // (Y * C)
    placed = (P("proto", None), P("batch", None), P("batch", None))
    return jax.shard_map(
        functools.partial(local, X, Z),
        mesh=mesh,
        in_specs=placed,
        out_specs=(P(("proto", "batch"), None), P("batch", None)),
        check_vma=False,
    )
```

```python
import functools
import math

import jax
import jax.numpy as jnp
from jax import lax
from jax.experimental import pallas as pl
from jax.experimental.pallas import tpu as pltpu
from jax.sharding import PartitionSpec as P

Y = 4
C = 2
LOG2E = 1.4426950408889634
TEACHER = LOG2E / 0.07
STUDENT = LOG2E / 0.1
LANES = 128
MESH = pl.DeviceIdType.MESH
NT = (((1,), (1,)), ((), ()))
F32 = jnp.float32
BF16 = jnp.bfloat16
GROUPS = 5
NARROW = (1, 2)


def dot_nt(a, b):
    return lax.dot_general(a, b, NT, preferred_element_type=F32)


def dot(a, b):
    return jnp.dot(a, b, preferred_element_type=F32)


def kernel(
    X, Z, p_hbm, te_hbm, se_hbm, out_hbm,
    p_v, te_all, se_all, ss, init, pe, sg, pt,
    tmx, tmx_r, pk_all, sst, sst_r, sg_all,
    csp, cs, cs_r, csc, rt, rt_r, rz, rz_r, af, bf,
    gacc, hx_s, hx_r, gsx_s, gsx_r, gxs_s, gxs_r, gsz_s, gsz_r, gszb_s, gszb_r, gsf,
    gpc_s, gpc_r, hy_s, hy_r, gy, gpy_s, gpy_r, gs_v,
    p_sem, o_sem, in_sem, out_sem, te_rs, se_rs, tx_rs, tz_rs, sx_rs, sz_rs, cs_rs, rx_rs, rz_rs,
    hx_rs, gx_rs, gxs_rs, gz_rs, gzb_rs, gf_rs, pc_rs, hy_rs, py_rs,
):
    b = lax.axis_index("batch")
    x = lax.axis_index("proto")
    z = b // (Y * C)
    y = (b // C) % Y
    c = b % C
    NP, D = p_v.shape
    KB = NP // Z
    T = KB // (Y * C)
    R = te_all.shape[1]
    NC = Z // 2
    NT8 = KB // T

    def dev(x_, z_, y_, c_):
        return {"batch": (z_ * Y + y_) * C + c_, "proto": x_}

    xs = [dev((x + d) % X, z, y, c) for d in range(X)]
    zs = [dev(x, (z + d) % Z, y, c) for d in range(Z)]
    ycs = [(dy, dc) for dc in range(C) for dy in range(Y)]
    yc = [dev(x, z, (y + dy) % Y, (c + dc) % C) for dy, dc in ycs]
    sent = [0] * GROUPS

    def send(src, dst, rsem, to, group):
        pltpu.make_async_remote_copy(
            src_ref=src, dst_ref=dst, send_sem=out_sem.at[group], recv_sem=rsem, device_id=to, device_id_type=MESH
        ).start()
        sent[group] += math.prod(src.shape) * src.dtype.itemsize

    def arrived(dst, rsem):
        pltpu.make_async_remote_copy(
            src_ref=dst, dst_ref=dst, send_sem=out_sem.at[0], recv_sem=rsem, device_id=xs[1], device_id_type=MESH
        ).wait_recv()

    own_t = pltpu.make_async_copy(te_hbm, te_all.at[z], o_sem.at[0])
    own_s = pltpu.make_async_copy(se_hbm, se_all.at[z], o_sem.at[1])
    own_t.start()
    own_s.start()

    def load(i):
        at = pl.multiple_of(i * KB, KB)
        return pltpu.make_async_copy(p_hbm.at[pl.ds(at, KB)], p_v.at[pl.ds(at, KB)], p_sem.at[i])

    ahead = min(4, Z)
    for i in range(2):
        load(i).start()
    barrier = pltpu.get_barrier_semaphore()
    near = (1, 2, 6, 7) if Z == 8 else range(1, Z)
    peers = xs[1:] + [zs[d] for d in near] + yc[1:]
    for peer in peers:
        pl.semaphore_signal(barrier, inc=1, device_id=peer, device_id_type=MESH)
    own_t.wait()
    own_s.wait()
    for i in range(2, ahead):
        load(i).start()

    HR = R // 2

    def gather_near(full, rs, group):
        if Z != 8:
            for d in range(1, Z):
                send(full.at[z], full.at[z], rs.at[4], zs[d], group)
            return
        for part in range(2):
            for d in (2, 6):
                low_half = (part == 0) == (d == 2)
                rows = pl.ds(0 if low_half else HR, HR)
                send(full.at[z, rows], full.at[z, rows], rs.at[part + (0 if d == 2 else 2)], zs[d], group)
        for d in (1, 7):
            send(full.at[z], full.at[z], rs.at[4], zs[d], group)

    def gather_far(full, rs, group):
        if Z != 8:
            return
        for part in range(2):
            for d in (2, 6):
                src = lax.rem(z + 8 - d, 8)
                low_half = (part == 0) == (d == 2)
                rows = pl.ds(0 if low_half else HR, HR)
                arrived(full.at[src, rows], rs.at[part + (0 if d == 2 else 2)])
                if part == 0:
                    send(full.at[src, rows], full.at[src, rows], rs.at[4], zs[d], group)
                send(full.at[src, rows], full.at[src, rows], rs.at[4], zs[1 if d == 2 else 7], group)

    def gather_end(full, rs):
        arrived(full.at[pl.ds(0, 5 if Z == 8 else Z - 1)], rs.at[4])

    own = jnp.concatenate([te_all[z], se_all[z]], axis=0)
    low = jnp.full((32, R), -jnp.inf, F32)

    def stats(i, carry, n=1):
        tm, sm = carry
        for k in range(n):
            load(i + k).wait()
        for k in range(n):

            @pl.when(i + k + ahead < Z)
            def _():
                load(i + k + ahead).start()

        at = pl.multiple_of(i * KB, KB)
        s = dot_nt(p_v[pl.ds(at, n * KB), :], own)
        ts = s[:, :R]
        st = s[:, R:]
        ss[pl.ds(at, n * KB), :] = st
        tm = jnp.maximum(tm, jnp.max(ts.reshape(n * KB // 32, 32, R), axis=0))
        sm = jnp.maximum(sm, jnp.max(st.reshape(n * KB // 32, 32, R), axis=0))
        return tm, sm

    def stats_pair(k, tops):
        return stats(2 * k, tops, 2)

    early = 1
    tops = lax.fori_loop(0, early, stats_pair, (low, low))
    pl.semaphore_wait(barrier, len(peers))
    if Z == 8:
        for d in (2, 6):
            pl.semaphore_signal(in_sem, inc=1, device_id=zs[d], device_id_type=MESH)
    gather_near(te_all, te_rs, 0)
    tops = lax.fori_loop(early, NC, stats_pair, tops)
    tmx[...] = jnp.max(tops[0], axis=0, keepdims=True) * TEACHER
    for d in range(1, X):
        send(tmx, tmx_r.at[d], tx_rs.at[0], xs[d], 4)

    s_top = jnp.max(tops[1], axis=0, keepdims=True) * STUDENT
    step = min(512, KB)

    def mass(k, acc):
        at = pl.multiple_of(k * step, step)
        e = jnp.exp2(ss[pl.ds(at, step), :] * STUDENT - s_top)
        return acc + jnp.sum(e.reshape(step // 32, 32, R), axis=0)

    half = NP // step // 2
    acc = lax.fori_loop(0, half, mass, jnp.zeros((32, R), F32))
    peak = tmx[...]
    arrived(tmx_r.at[pl.ds(1, X - 1)], tx_rs.at[0])
    for d in range(1, X):
        peak = jnp.maximum(peak, tmx_r[d])
    if Z == 8:
        pl.semaphore_wait(in_sem, 2)
    pk_all[z] = peak
    for d in range(1, Z):
        send(pk_all.at[z], pk_all.at[z], tz_rs.at[0], zs[d], 4)
    gather_far(te_all, te_rs, 0)
    acc = lax.fori_loop(half, NP // step, mass, acc)
    sst[0] = s_top
    sst[1] = jnp.sum(acc, axis=0, keepdims=True)
    for d in range(1, X):
        send(sst, sst_r.at[d], sx_rs.at[0], xs[d], 4)
    for k in range(NT8):
        tile = p_v[pl.ds(pl.multiple_of(z * KB + k * T, T), T), :]
        pt[:, k * T : (k + 1) * T] = tile.T
    arrived(pk_all.at[pl.ds(0, Z - 1)], tz_rs.at[0])
    gather_end(te_all, te_rs)
    gather_near(se_all, se_rs, 1)

    def pair(ref, j):
        return jnp.concatenate([ref[2 * j], ref[2 * j + 1]], axis=0)

    def row_pair(ref, j):
        return jnp.concatenate([ref[2 * j], ref[2 * j + 1]], axis=1)

    block = p_v.at[pl.ds(pl.multiple_of(z * KB, KB), KB)]
    for j in range(NC):
        e = jnp.exp2(dot_nt(block[...], pair(te_all, j)) * TEACHER - row_pair(pk_all, j))
        init[j] = e
        e = e[:, :R] + e[:, R:]
        csp[...] = e if j == 0 else csp[...] + e
    for h in range(KB // LANES):
        cs[h] = jnp.sum(csp[h * LANES : (h + 1) * LANES].T, axis=0, keepdims=True)
    for i in range(1, Y * C):
        send(cs, cs_r.at[i], cs_rs.at[0], yc[i], 0)
    arrived(sst_r.at[pl.ds(1, X - 1)], sx_rs.at[0])
    top = sst[0]
    for d in range(1, X):
        top = jnp.maximum(top, sst_r[d, 0])
    total = sst[1] * jnp.exp2(sst[0] - top)
    for d in range(1, X):
        total = total + sst_r[d, 1] * jnp.exp2(sst_r[d, 0] - top)
    sg_all[z, 0] = top
    sg_all[z, 1] = total
    for d in range(1, Z):
        send(sg_all.at[z], sg_all.at[z], sz_rs.at[0], zs[d], 4)
    gather_far(se_all, se_rs, 1)
    tot = cs[...]
    arrived(cs_r.at[pl.ds(1, Y * C - 1)], cs_rs.at[0])
    for i in range(1, Y * C):
        tot = tot + cs_r[i]
    csc[...] = 1.0 / tot

    def rows(k, accs):
        at = pl.multiple_of(k * LANES, LANES)
        scale = jnp.broadcast_to(csc[k], (LANES, LANES)).T
        out = []
        for j in range(NC):
            for h in range(2):
                v = init[j, pl.ds(at, LANES), h * R : (h + 1) * R] * scale
                init[j, pl.ds(at, LANES), h * R : (h + 1) * R] = v
                out.append(accs[2 * j + h] + jnp.sum(v.reshape(LANES // 8, 8, R), axis=0))
        return tuple(out)

    accs = lax.fori_loop(0, KB // LANES, rows, tuple(jnp.zeros((8, R), F32) for _ in range(Z)), unroll=8)
    for i in range(Z):
        rt[i] = jnp.sum(accs[i], axis=0, keepdims=True)
    for d in range(1, X):
        send(rt, rt_r.at[d], rx_rs.at[0], xs[d], 0)

    def learn(j):
        tops_j = jnp.concatenate([sg_all[2 * j, 0], sg_all[2 * j + 1, 0]], axis=1)
        pe[j] = jnp.exp2(dot_nt(block[...], pair(se_all, j)) * STUDENT - tops_j) * row_pair(af, j)

    tot = rt[...]
    arrived(rt_r.at[pl.ds(1, X - 1)], rx_rs.at[0])
    for d in range(1, X):
        tot = tot + rt_r[d]
    rz[...] = tot
    for d in range(1, Z):
        send(rz, rz_r.at[d], rz_rs.at[0], zs[d], 0)
    gather_end(se_all, se_rs)
    arrived(sg_all.at[pl.ds(0, Z - 1)], sz_rs.at[0])
    for i in range(Z):
        af[i] = 10.0 / sg_all[i, 1]
    for j in range(NC):
        learn(j)
    tot = rz[...]
    arrived(rz_r.at[pl.ds(1, Z - 1)], rz_rs.at[0])
    for d in range(1, Z):
        tot = tot + rz_r[d]
    bf[...] = 10.0 / tot

    Q = D // X
    HQ = Q // 2
    HT = T // 2
    narrow = NARROW if NC == 4 else ()
    order = [2, 1, 3, 0] if NC == 4 else list(range(1, NC)) + [0]

    def piece(o, d):
        return gacc.at[o, lax.rem(x + d, X)]

    def x_relayed(o):
        for side in range(2):
            to = xs[1 if side == 0 else 3]
            hx_s[o, side] = piece(o, 2)[side * HQ : (side + 1) * HQ].astype(BF16)
            send(hx_s.at[o, side], hx_r.at[o, side], hx_rs.at[o], to, 2)

    def x_direct(o):
        for side in range(2):
            to = xs[1 if side == 0 else 3]
            at = (1 - side) * HQ
            gsx_s[o, side] = piece(o, 1 if side == 0 else 3)[at : at + HQ].astype(BF16)
            send(gsx_s.at[o, side], gsx_r.at[o, side], gx_rs.at[o], to, 2)

    def x_second(o):
        arrived(hx_r.at[o], hx_rs.at[o])
        for side in range(2):
            at = side * HQ
            gxs_s[o, side] = piece(o, 1 if side == 0 else 3)[at : at + HQ] + hx_r[o, side].astype(F32)
            send(gxs_s.at[o, side], gxs_r.at[o, side], gxs_rs.at[o], xs[1 if side == 0 else 3], 2)

    def x_third(o):
        j = lax.rem(z // 2 + o, NC)
        arrived(gsx_r.at[o], gx_rs.at[o])
        arrived(gxs_r.at[o], gxs_rs.at[o])
        keep, there, rsem = (gszb_s, gszb_r, gzb_rs) if o in narrow else (gsz_s, gsz_r, gz_rs)
        for part in range(2):
            at = part * HQ
            tot = piece(o, 0)[at : at + HQ] + gxs_r[o, part] + gsx_r[o, 1 - part].astype(F32)
            for h in range(2):
                keep[o, h, at : at + HQ] = tot[:, h * R : (h + 1) * R].astype(keep.dtype)
        for h in range(1 if o == 0 else 2):
            to = 1 - z % 2 if o == 0 else h
            send(keep.at[o, to], there.at[z], rsem.at[0], dev(x, 2 * j + to, y, c), 2)

    for n in range(0, NC, 2):
        group = order[n : n + 2]
        gs = []
        for o in group:
            j = lax.rem(z // 2 + o, NC)
            g = (pe[j] - init[j] * row_pair(bf, j)).astype(BF16)
            sg[j] = g
            gs.append(g)
        acc = dot(pt[...], jnp.concatenate(gs, axis=1))
        for i, o in enumerate(group):
            for q in range(X):
                gacc[o, q] = acc[q * Q : (q + 1) * Q, i * 2 * R : (i + 1) * 2 * R]
            x_relayed(o)

    for o in order:
        x_direct(o)

    def proto_tiles(deltas, c_):
        lhs = []
        for d in deltas:
            at = pl.multiple_of((lax.rem(y + d, Y) * C + c_) * T, T)
            lhs.append(jnp.concatenate([sg[j, pl.ds(at, T), :] for j in range(NC)], axis=1))
        return dot(jnp.concatenate(lhs, axis=0), se_all[...].reshape(Z * R, D))

    partner = yc[Y]

    def to_partner(n, deltas):
        g = proto_tiles(deltas, 1 - c)
        for i in range(len(deltas)):
            gpc_s[n + i] = g[i * T : (i + 1) * T]
        send(gpc_s.at[pl.ds(n, len(deltas))], gpc_r.at[pl.ds(n, len(deltas))], pc_rs.at[n], partner, 3)

    def to_y(side, part, value):
        gpy_s[side, part] = value.astype(BF16)
        send(gpy_s.at[side, part], gpy_r.at[side, part], py_rs.at[0], yc[1 if side == 0 else 3], 3)

    steps = [("s", o) for o in order] + [("t", o) for o in order]

    def advance(count):
        for _ in range(min(count, len(steps))):
            kind, o = steps.pop(0)
            (x_second if kind == "s" else x_third)(o)

    to_partner(0, (2,))
    to_partner(1, (1, 3))
    advance(1)
    g = proto_tiles((2,), c)
    advance(3)
    arrived(gpc_r.at[pl.ds(0, 1)], pc_rs.at[0])
    for side in range(2):
        at = side * HT
        hy_s[side] = (g[at : at + HT] + gpc_r[0, at : at + HT]).astype(BF16)
        send(hy_s.at[side], hy_r.at[side], hy_rs.at[0], yc[1 if side == 0 else 3], 3)
    to_partner(3, (0,))
    g = proto_tiles((1, 3), c)
    advance(2)
    arrived(gpc_r.at[pl.ds(1, 2)], pc_rs.at[1])
    to_y(0, 1, g[HT:T] + gpc_r[1, HT:])
    gy[0] = g[:HT] + gpc_r[1, :HT]
    to_y(1, 0, g[T : T + HT] + gpc_r[2, :HT])
    gy[1] = g[T + HT :] + gpc_r[2, HT:]
    advance(len(steps))
    g = proto_tiles((0,), c)
    gy[2] = g[:HT]
    gy[3] = g[HT:]
    arrived(hy_r, hy_rs.at[0])
    to_y(0, 0, gy[0] + hy_r[0].astype(F32))
    to_y(1, 1, gy[1] + hy_r[1].astype(F32))
    arrived(gsz_r.at[pl.ds(0, Z - 1 - 2 * len(narrow))], gz_rs.at[0])
    if narrow:
        arrived(gszb_r.at[pl.ds(0, 2 * len(narrow))], gzb_rs.at[0])
    tot = gsz_s[0, z % 2]
    tot = tot + gsz_r[z + 1 - 2 * (z % 2)]
    for o in range(1, NC):
        j = lax.rem(z // 2 + o, NC)
        for h in range(2):
            tot = tot + (gszb_r if NC - o in narrow else gsz_r)[2 * j + h].astype(F32)
    gsf[x] = tot
    for d in range(1, X):
        send(gsf.at[x], gsf.at[x], gf_rs.at[0], xs[d], 3)
    arrived(gpy_r, py_rs.at[0])
    arrived(gpc_r.at[pl.ds(3, 1)], pc_rs.at[3])
    for part in range(2):
        tot = gy[2 + part] + gpc_r[3, part * HT : (part + 1) * HT]
        for side in range(2):
            tot = tot + gpy_r[side, part].astype(F32)
        gy[2 + part] = tot
    outs = [
        pltpu.make_async_copy(gy.at[2 + part], out_hbm.at[pl.ds(part * HT, HT)], o_sem.at[part])
        for part in range(2)
    ]
    for out in outs:
        out.start()
    arrived(gsf.at[pl.ds(0, X - 1)], gf_rs.at[0])
    full = gsf[...].reshape(D, R)
    for h in range(D // LANES):
        gs_v[:, h * LANES : (h + 1) * LANES] = full[h * LANES : (h + 1) * LANES].T
    out = pltpu.make_async_copy(gs_v, out_hbm.at[pl.ds(T, R)], o_sem.at[2])
    out.start()
    outs.append(out)
    for group, size in enumerate(sent):
        n = size // (2 * D)
        whole = cs_r.at[pl.ds(0, 2), pl.ds(0, n // 2)] if group == 4 else p_v.at[pl.ds(0, n)]
        pltpu.make_async_remote_copy(
            src_ref=whole, dst_ref=whole, send_sem=out_sem.at[group],
            recv_sem=tx_rs.at[0], device_id=xs[1], device_id_type=MESH,
        ).wait_send()
    for out in outs:
        out.wait()


def split(in_hbm, gp_hbm, gs_hbm, buf, i_sem, o_sem):
    T = gp_hbm.shape[0]
    R = gs_hbm.shape[0]
    ins = [
        pltpu.make_async_copy(in_hbm.at[pl.ds(at, n)], buf.at[pl.ds(at, n)], i_sem.at[k])
        for k, (at, n) in enumerate(((0, T), (T, R)))
    ]
    outs = [
        pltpu.make_async_copy(buf.at[pl.ds(0, T)], gp_hbm, o_sem.at[0]),
        pltpu.make_async_copy(buf.at[pl.ds(T, R)], gs_hbm, o_sem.at[1]),
    ]
    for copy in ins:
        copy.start()
    for copy, out in zip(ins, outs):
        copy.wait()
        out.start()
    for out in outs:
        out.wait()


def local(X, Z, prototypes, teacher_embed, student_embed):
    NP, D = prototypes.shape
    R = teacher_embed.shape[0]
    KB = NP // Z
    T = KB // (Y * C)
    NC = Z // 2
    Q = D // X
    HQ = Q // 2
    HT = T // 2
    V = pltpu.VMEM
    dma = pltpu.SemaphoreType.DMA
    hbm = pl.BlockSpec(memory_space=pl.ANY)
    scratch = [
        V((NP, D), BF16), V((Z, R, D), BF16), V((Z, R, D), BF16), V((NP, R), F32),
        V((NC, KB, 2 * R), F32), V((NC, KB, 2 * R), F32), V((NC, KB, 2 * R), BF16), V((D, KB), BF16),
        V((1, R), F32), V((X, 1, R), F32), V((Z, 1, R), F32),
        V((2, 1, R), F32), V((X, 2, 1, R), F32), V((Z, 2, 1, R), F32),
        V((KB, R), F32), V((KB // LANES, 1, LANES), F32), V((Y * C, KB // LANES, 1, LANES), F32),
        V((KB // LANES, 1, LANES), F32),
        V((Z, 1, R), F32), V((X, Z, 1, R), F32), V((Z, 1, R), F32), V((Z, Z, 1, R), F32),
        V((Z, 1, R), F32), V((Z, 1, R), F32),
        V((NC, X, Q, 2 * R), F32), V((NC, 2, HQ, 2 * R), BF16), V((NC, 2, HQ, 2 * R), BF16),
        V((NC, 2, HQ, 2 * R), BF16), V((NC, 2, HQ, 2 * R), BF16), V((NC, 2, HQ, 2 * R), F32), V((NC, 2, HQ, 2 * R), F32),
        V((NC, 2, Q, R), F32), V((Z, Q, R), F32), V((NC, 2, Q, R), BF16), V((Z, Q, R), BF16), V((X, Q, R), F32),
        V((Y, T, D), F32), V((Y, T, D), F32), V((2, HT, D), BF16), V((2, HT, D), BF16), V((4, HT, D), F32),
        V((2, 2, HT, D), BF16), V((2, 2, HT, D), BF16), V((R, D), F32),
        dma((Z,)), dma((3,)), pltpu.SemaphoreType.REGULAR, dma((GROUPS,)), dma((5,)), dma((5,)), *[dma((1,))] * 7,
        dma((NC,)), dma((NC,)), dma((NC,)), dma((1,)), dma((1,)), dma((1,)), dma((Y,)), dma((1,)), dma((1,)),
    ]
    out = pl.pallas_call(
        functools.partial(kernel, X, Z),
        out_shape=jax.ShapeDtypeStruct((T + R, D), F32),
        in_specs=[hbm, hbm, hbm],
        out_specs=hbm,
        scratch_shapes=scratch,
        compiler_params=pltpu.CompilerParams(
            collective_id=0, has_side_effects=True, vmem_limit_bytes=63 << 20
        ),
        name="head",
    )(prototypes, teacher_embed, student_embed)
    return pl.pallas_call(
        split,
        out_shape=(jax.ShapeDtypeStruct((T, D), F32), jax.ShapeDtypeStruct((R, D), F32)),
        in_specs=[hbm],
        out_specs=(hbm, hbm),
        scratch_shapes=[V((T + R, D), F32), dma((2,)), dma((2,))],
        name="split",
    )(out)


def solution(mesh):
    X = mesh.shape["proto"]
    Z = mesh.shape["batch"] // (Y * C)
    placed = (P("proto", None), P("batch", None), P("batch", None))
    return jax.shard_map(
        functools.partial(local, X, Z),
        mesh=mesh,
        in_specs=placed,
        out_specs=(P(("proto", "batch"), None), P("batch", None)),
        check_vma=False,
    )
```

```python
import functools
import math

import jax
import jax.numpy as jnp
from jax import lax
from jax.experimental import pallas as pl
from jax.experimental.pallas import tpu as pltpu
from jax.sharding import PartitionSpec as P

Y = 4
C = 2
LOG2E = 1.4426950408889634
TEACHER = LOG2E / 0.07
STUDENT = LOG2E / 0.1
LANES = 128
MESH = pl.DeviceIdType.MESH
NT = (((1,), (1,)), ((), ()))
F32 = jnp.float32
BF16 = jnp.bfloat16
GROUPS = 5
NARROW = (1, 2)


def dot_nt(a, b):
    return lax.dot_general(a, b, NT, preferred_element_type=F32)


def dot(a, b):
    return jnp.dot(a, b, preferred_element_type=F32)


def kernel(
    X, Z, p_hbm, te_hbm, se_hbm, out_hbm,
    p_v, te_all, se_all, ss, init, pe, sg, pt,
    tmx, tmx_r, pk_all, sst, sst_r, sg_all,
    csp, cs, cs_r, csc, rt, rt_r, rz, rz_r, af, bf,
    gacc, hx_s, hx_r, gsx_s, gsx_r, gxs_s, gxs_r, gsz_s, gsz_r, gszb_s, gszb_r, gsf,
    gpc_s, gpc_r, hy_s, hy_r, gy, gpy_s, gpy_r, gs_v,
    p_sem, o_sem, in_sem, out_sem, te_rs, se_rs, tx_rs, tz_rs, sx_rs, sz_rs, cs_rs, rx_rs, rz_rs,
    hx_rs, gx_rs, gxs_rs, gz_rs, gzb_rs, gf_rs, pc_rs, hy_rs, py_rs,
):
    b = lax.axis_index("batch")
    x = lax.axis_index("proto")
    z = b // (Y * C)
    y = (b // C) % Y
    c = b % C
    NP, D = p_v.shape
    KB = NP // Z
    T = KB // (Y * C)
    R = te_all.shape[1]
    NC = Z // 2
    NT8 = KB // T

    def dev(x_, z_, y_, c_):
        return {"batch": (z_ * Y + y_) * C + c_, "proto": x_}

    xs = [dev((x + d) % X, z, y, c) for d in range(X)]
    zs = [dev(x, (z + d) % Z, y, c) for d in range(Z)]
    far_x = sorted(range(1, X), key=lambda d: -min(d, X - d))
    far_z = sorted(range(1, Z), key=lambda d: -min(d, Z - d))
    far_yc = sorted(range(1, Y * C), key=lambda i: -min(i % Y, Y - i % Y))
    ycs = [(dy, dc) for dc in range(C) for dy in range(Y)]
    yc = [dev(x, z, (y + dy) % Y, (c + dc) % C) for dy, dc in ycs]
    sent = [0] * GROUPS

    def send(src, dst, rsem, to, group):
        pltpu.make_async_remote_copy(
            src_ref=src, dst_ref=dst, send_sem=out_sem.at[group], recv_sem=rsem, device_id=to, device_id_type=MESH
        ).start()
        sent[group] += math.prod(src.shape) * src.dtype.itemsize

    def arrived(dst, rsem):
        pltpu.make_async_remote_copy(
            src_ref=dst, dst_ref=dst, send_sem=out_sem.at[0], recv_sem=rsem, device_id=xs[1], device_id_type=MESH
        ).wait_recv()

    own_t = pltpu.make_async_copy(te_hbm, te_all.at[z], o_sem.at[0])
    own_s = pltpu.make_async_copy(se_hbm, se_all.at[z], o_sem.at[1])
    own_t.start()
    own_s.start()

    def load(i):
        at = pl.multiple_of(i * KB, KB)
        return pltpu.make_async_copy(p_hbm.at[pl.ds(at, KB)], p_v.at[pl.ds(at, KB)], p_sem.at[i])

    ahead = min(4, Z)
    for i in range(2):
        load(i).start()
    barrier = pltpu.get_barrier_semaphore()
    near = (1, 2, 6, 7) if Z == 8 else range(1, Z)
    peers = xs[1:] + [zs[d] for d in near] + yc[1:]
    for peer in peers:
        pl.semaphore_signal(barrier, inc=1, device_id=peer, device_id_type=MESH)
    own_t.wait()
    own_s.wait()
    for i in range(2, ahead):
        load(i).start()

    HR = R // 2

    def gather_near(full, rs, group):
        if Z != 8:
            for d in range(1, Z):
                send(full.at[z], full.at[z], rs.at[4], zs[d], group)
            return
        for part in range(2):
            for d in (2, 6):
                low_half = (part == 0) == (d == 2)
                rows = pl.ds(0 if low_half else HR, HR)
                send(full.at[z, rows], full.at[z, rows], rs.at[part + (0 if d == 2 else 2)], zs[d], group)
        for d in (1, 7):
            send(full.at[z], full.at[z], rs.at[4], zs[d], group)

    def gather_far(full, rs, group):
        if Z != 8:
            return
        for part in range(2):
            for d in (2, 6):
                src = lax.rem(z + 8 - d, 8)
                low_half = (part == 0) == (d == 2)
                rows = pl.ds(0 if low_half else HR, HR)
                arrived(full.at[src, rows], rs.at[part + (0 if d == 2 else 2)])
                if part == 0:
                    send(full.at[src, rows], full.at[src, rows], rs.at[4], zs[d], group)
                send(full.at[src, rows], full.at[src, rows], rs.at[4], zs[1 if d == 2 else 7], group)

    def gather_end(full, rs):
        arrived(full.at[pl.ds(0, 5 if Z == 8 else Z - 1)], rs.at[4])

    own = jnp.concatenate([te_all[z], se_all[z]], axis=0)
    low = jnp.full((32, R), -jnp.inf, F32)

    def stats(i, carry, n=1):
        tm, sm = carry
        for k in range(n):
            load(i + k).wait()
        for k in range(n):

            @pl.when(i + k + ahead < Z)
            def _():
                load(i + k + ahead).start()

        at = pl.multiple_of(i * KB, KB)
        s = dot_nt(p_v[pl.ds(at, n * KB), :], own)
        ts = s[:, :R]
        st = s[:, R:]
        ss[pl.ds(at, n * KB), :] = st
        tm = jnp.maximum(tm, jnp.max(ts.reshape(n * KB // 32, 32, R), axis=0))
        sm = jnp.maximum(sm, jnp.max(st.reshape(n * KB // 32, 32, R), axis=0))
        return tm, sm

    def stats_pair(k, tops):
        return stats(2 * k, tops, 2)

    early = 1
    tops = lax.fori_loop(0, early, stats_pair, (low, low))
    pl.semaphore_wait(barrier, len(peers))
    if Z == 8:
        for d in (2, 6):
            pl.semaphore_signal(in_sem, inc=1, device_id=zs[d], device_id_type=MESH)
    gather_near(te_all, te_rs, 0)
    tops = lax.fori_loop(early, NC, stats_pair, tops)
    tmx[...] = jnp.max(tops[0], axis=0, keepdims=True) * TEACHER
    for d in far_x:
        send(tmx, tmx_r.at[d], tx_rs.at[0], xs[d], 4)

    s_top = jnp.max(tops[1], axis=0, keepdims=True) * STUDENT
    step = min(512, KB)

    def mass(k, acc):
        at = pl.multiple_of(k * step, step)
        e = jnp.exp2(ss[pl.ds(at, step), :] * STUDENT - s_top)
        return acc + jnp.sum(e.reshape(step // 32, 32, R), axis=0)

    half = NP // step // 2
    acc = lax.fori_loop(0, half, mass, jnp.zeros((32, R), F32))
    peak = tmx[...]
    arrived(tmx_r.at[pl.ds(1, X - 1)], tx_rs.at[0])
    for d in range(1, X):
        peak = jnp.maximum(peak, tmx_r[d])
    if Z == 8:
        pl.semaphore_wait(in_sem, 2)
    pk_all[z] = peak
    for d in far_z:
        send(pk_all.at[z], pk_all.at[z], tz_rs.at[0], zs[d], 4)
    gather_far(te_all, te_rs, 0)
    acc = lax.fori_loop(half, NP // step, mass, acc)
    sst[0] = s_top
    sst[1] = jnp.sum(acc, axis=0, keepdims=True)
    for d in range(1, X):
        send(sst, sst_r.at[d], sx_rs.at[0], xs[d], 4)
    for k in range(NT8):
        tile = p_v[pl.ds(pl.multiple_of(z * KB + k * T, T), T), :]
        pt[:, k * T : (k + 1) * T] = tile.T
    arrived(pk_all.at[pl.ds(0, Z - 1)], tz_rs.at[0])
    gather_end(te_all, te_rs)
    gather_near(se_all, se_rs, 1)

    def pair(ref, j):
        return jnp.concatenate([ref[2 * j], ref[2 * j + 1]], axis=0)

    def row_pair(ref, j):
        return jnp.concatenate([ref[2 * j], ref[2 * j + 1]], axis=1)

    block = p_v.at[pl.ds(pl.multiple_of(z * KB, KB), KB)]
    for j in range(NC):
        e = jnp.exp2(dot_nt(block[...], pair(te_all, j)) * TEACHER - row_pair(pk_all, j))
        init[j] = e
        e = e[:, :R] + e[:, R:]
        csp[...] = e if j == 0 else csp[...] + e
    for h in range(KB // LANES):
        cs[h] = jnp.sum(csp[h * LANES : (h + 1) * LANES].T, axis=0, keepdims=True)
    for i in far_yc:
        send(cs, cs_r.at[i], cs_rs.at[0], yc[i], 0)
    arrived(sst_r.at[pl.ds(1, X - 1)], sx_rs.at[0])
    top = sst[0]
    for d in range(1, X):
        top = jnp.maximum(top, sst_r[d, 0])
    total = sst[1] * jnp.exp2(sst[0] - top)
    for d in range(1, X):
        total = total + sst_r[d, 1] * jnp.exp2(sst_r[d, 0] - top)
    sg_all[z, 0] = top
    sg_all[z, 1] = total
    for d in range(1, Z):
        send(sg_all.at[z], sg_all.at[z], sz_rs.at[0], zs[d], 4)
    gather_far(se_all, se_rs, 1)
    tot = cs[...]
    arrived(cs_r.at[pl.ds(1, Y * C - 1)], cs_rs.at[0])
    for i in range(1, Y * C):
        tot = tot + cs_r[i]
    csc[...] = 1.0 / tot

    def rows(k, accs):
        at = pl.multiple_of(k * LANES, LANES)
        scale = jnp.broadcast_to(csc[k], (LANES, LANES)).T
        out = []
        for j in range(NC):
            for h in range(2):
                v = init[j, pl.ds(at, LANES), h * R : (h + 1) * R] * scale
                init[j, pl.ds(at, LANES), h * R : (h + 1) * R] = v
                out.append(accs[2 * j + h] + jnp.sum(v.reshape(LANES // 8, 8, R), axis=0))
        return tuple(out)

    accs = lax.fori_loop(0, KB // LANES, rows, tuple(jnp.zeros((8, R), F32) for _ in range(Z)), unroll=8)
    for i in range(Z):
        rt[i] = jnp.sum(accs[i], axis=0, keepdims=True)
    for d in far_x:
        send(rt, rt_r.at[d], rx_rs.at[0], xs[d], 0)

    def learn(j):
        tops_j = jnp.concatenate([sg_all[2 * j, 0], sg_all[2 * j + 1, 0]], axis=1)
        pe[j] = jnp.exp2(dot_nt(block[...], pair(se_all, j)) * STUDENT - tops_j) * row_pair(af, j)

    tot = rt[...]
    arrived(rt_r.at[pl.ds(1, X - 1)], rx_rs.at[0])
    for d in range(1, X):
        tot = tot + rt_r[d]
    rz[...] = tot
    for d in far_z:
        send(rz, rz_r.at[d], rz_rs.at[0], zs[d], 0)
    gather_end(se_all, se_rs)
    arrived(sg_all.at[pl.ds(0, Z - 1)], sz_rs.at[0])
    for i in range(Z):
        af[i] = 10.0 / sg_all[i, 1]
    for j in range(NC):
        learn(j)
    tot = rz[...]
    arrived(rz_r.at[pl.ds(1, Z - 1)], rz_rs.at[0])
    for d in range(1, Z):
        tot = tot + rz_r[d]
    bf[...] = 10.0 / tot

    Q = D // X
    HQ = Q // 2
    HT = T // 2
    narrow = NARROW if NC == 4 else ()
    order = [2, 1, 3, 0] if NC == 4 else list(range(1, NC)) + [0]

    def piece(o, d):
        return gacc.at[o, lax.rem(x + d, X)]

    def x_relayed(o):
        for side in range(2):
            to = xs[1 if side == 0 else 3]
            hx_s[o, side] = piece(o, 2)[side * HQ : (side + 1) * HQ].astype(BF16)
            send(hx_s.at[o, side], hx_r.at[o, side], hx_rs.at[o], to, 2)

    def x_direct(o):
        for side in range(2):
            to = xs[1 if side == 0 else 3]
            at = (1 - side) * HQ
            gsx_s[o, side] = piece(o, 1 if side == 0 else 3)[at : at + HQ].astype(BF16)
            send(gsx_s.at[o, side], gsx_r.at[o, side], gx_rs.at[o], to, 2)

    def x_second(o):
        arrived(hx_r.at[o], hx_rs.at[o])
        for side in range(2):
            at = side * HQ
            gxs_s[o, side] = piece(o, 1 if side == 0 else 3)[at : at + HQ] + hx_r[o, side].astype(F32)
            send(gxs_s.at[o, side], gxs_r.at[o, side], gxs_rs.at[o], xs[1 if side == 0 else 3], 2)

    def x_third(o):
        j = lax.rem(z // 2 + o, NC)
        arrived(gsx_r.at[o], gx_rs.at[o])
        arrived(gxs_r.at[o], gxs_rs.at[o])
        keep, there, rsem = (gszb_s, gszb_r, gzb_rs) if o in narrow else (gsz_s, gsz_r, gz_rs)
        for part in range(2):
            at = part * HQ
            tot = piece(o, 0)[at : at + HQ] + gxs_r[o, part] + gsx_r[o, 1 - part].astype(F32)
            for h in range(2):
                keep[o, h, at : at + HQ] = tot[:, h * R : (h + 1) * R].astype(keep.dtype)
        for h in range(1 if o == 0 else 2):
            to = 1 - z % 2 if o == 0 else h
            send(keep.at[o, to], there.at[z], rsem.at[0], dev(x, 2 * j + to, y, c), 2)

    for n in range(0, NC, 2):
        group = order[n : n + 2]
        gs = []
        for o in group:
            j = lax.rem(z // 2 + o, NC)
            g = (pe[j] - init[j] * row_pair(bf, j)).astype(BF16)
            sg[j] = g
            gs.append(g)
        acc = dot(pt[...], jnp.concatenate(gs, axis=1))
        for i, o in enumerate(group):
            for q in range(X):
                gacc[o, q] = acc[q * Q : (q + 1) * Q, i * 2 * R : (i + 1) * 2 * R]
            x_relayed(o)

    for o in order:
        x_direct(o)

    def proto_tiles(deltas, c_):
        lhs = []
        for d in deltas:
            at = pl.multiple_of((lax.rem(y + d, Y) * C + c_) * T, T)
            lhs.append(jnp.concatenate([sg[j, pl.ds(at, T), :] for j in range(NC)], axis=1))
        return dot(jnp.concatenate(lhs, axis=0), se_all[...].reshape(Z * R, D))

    partner = yc[Y]

    def to_partner(n, deltas):
        g = proto_tiles(deltas, 1 - c)
        for i in range(len(deltas)):
            gpc_s[n + i] = g[i * T : (i + 1) * T]
        send(gpc_s.at[pl.ds(n, len(deltas))], gpc_r.at[pl.ds(n, len(deltas))], pc_rs.at[n], partner, 3)

    def to_y(side, part, value):
        gpy_s[side, part] = value.astype(BF16)
        send(gpy_s.at[side, part], gpy_r.at[side, part], py_rs.at[0], yc[1 if side == 0 else 3], 3)

    steps = [("s", o) for o in order] + [("t", o) for o in order]

    def advance(count):
        for _ in range(min(count, len(steps))):
            kind, o = steps.pop(0)
            (x_second if kind == "s" else x_third)(o)

    to_partner(0, (2,))
    to_partner(1, (1, 3))
    advance(1)
    g = proto_tiles((2,), c)
    advance(3)
    arrived(gpc_r.at[pl.ds(0, 1)], pc_rs.at[0])
    for side in range(2):
        at = side * HT
        hy_s[side] = (g[at : at + HT] + gpc_r[0, at : at + HT]).astype(BF16)
        send(hy_s.at[side], hy_r.at[side], hy_rs.at[0], yc[1 if side == 0 else 3], 3)
    to_partner(3, (0,))
    g = proto_tiles((1, 3), c)
    advance(2)
    arrived(gpc_r.at[pl.ds(1, 2)], pc_rs.at[1])
    to_y(0, 1, g[HT:T] + gpc_r[1, HT:])
    gy[0] = g[:HT] + gpc_r[1, :HT]
    to_y(1, 0, g[T : T + HT] + gpc_r[2, :HT])
    gy[1] = g[T + HT :] + gpc_r[2, HT:]
    advance(len(steps))
    g = proto_tiles((0,), c)
    gy[2] = g[:HT]
    gy[3] = g[HT:]
    arrived(hy_r, hy_rs.at[0])
    to_y(0, 0, gy[0] + hy_r[0].astype(F32))
    to_y(1, 1, gy[1] + hy_r[1].astype(F32))
    arrived(gsz_r.at[pl.ds(0, Z - 1 - 2 * len(narrow))], gz_rs.at[0])
    if narrow:
        arrived(gszb_r.at[pl.ds(0, 2 * len(narrow))], gzb_rs.at[0])
    tot = gsz_s[0, z % 2]
    tot = tot + gsz_r[z + 1 - 2 * (z % 2)]
    for o in range(1, NC):
        j = lax.rem(z // 2 + o, NC)
        for h in range(2):
            tot = tot + (gszb_r if NC - o in narrow else gsz_r)[2 * j + h].astype(F32)
    gsf[x] = tot
    for d in far_x:
        send(gsf.at[x], gsf.at[x], gf_rs.at[0], xs[d], 3)
    arrived(gpy_r, py_rs.at[0])
    arrived(gpc_r.at[pl.ds(3, 1)], pc_rs.at[3])
    for part in range(2):
        tot = gy[2 + part] + gpc_r[3, part * HT : (part + 1) * HT]
        for side in range(2):
            tot = tot + gpy_r[side, part].astype(F32)
        out_hbm[pl.ds(part * HT, HT), :] = tot
    arrived(gsf.at[pl.ds(0, X - 1)], gf_rs.at[0])
    full = gsf[...].reshape(D, R)
    for h in range(D // LANES):
        out_hbm[pl.ds(T, R), h * LANES : (h + 1) * LANES] = full[h * LANES : (h + 1) * LANES].T
    for group, size in enumerate(sent):
        n = size // (2 * D)
        whole = cs_r.at[pl.ds(0, 2), pl.ds(0, n // 2)] if group == 4 else p_v.at[pl.ds(0, n)]
        pltpu.make_async_remote_copy(
            src_ref=whole, dst_ref=whole, send_sem=out_sem.at[group],
            recv_sem=tx_rs.at[0], device_id=xs[1], device_id_type=MESH,
        ).wait_send()


def split(in_v, gp_hbm, gs_hbm, o_sem):
    T = gp_hbm.shape[0]
    R = gs_hbm.shape[0]
    outs = [
        pltpu.make_async_copy(in_v.at[pl.ds(0, T)], gp_hbm, o_sem.at[0]),
        pltpu.make_async_copy(in_v.at[pl.ds(T, R)], gs_hbm, o_sem.at[1]),
    ]
    for out in outs:
        out.start()
    for out in outs:
        out.wait()


def local(X, Z, prototypes, teacher_embed, student_embed):
    NP, D = prototypes.shape
    R = teacher_embed.shape[0]
    KB = NP // Z
    T = KB // (Y * C)
    NC = Z // 2
    Q = D // X
    HQ = Q // 2
    HT = T // 2
    V = pltpu.VMEM
    dma = pltpu.SemaphoreType.DMA
    hbm = pl.BlockSpec(memory_space=pl.ANY)
    scratch = [
        V((NP, D), BF16), V((Z, R, D), BF16), V((Z, R, D), BF16), V((NP, R), F32),
        V((NC, KB, 2 * R), F32), V((NC, KB, 2 * R), F32), V((NC, KB, 2 * R), BF16), V((D, KB), BF16),
        V((1, R), F32), V((X, 1, R), F32), V((Z, 1, R), F32),
        V((2, 1, R), F32), V((X, 2, 1, R), F32), V((Z, 2, 1, R), F32),
        V((KB, R), F32), V((KB // LANES, 1, LANES), F32), V((Y * C, KB // LANES, 1, LANES), F32),
        V((KB // LANES, 1, LANES), F32),
        V((Z, 1, R), F32), V((X, Z, 1, R), F32), V((Z, 1, R), F32), V((Z, Z, 1, R), F32),
        V((Z, 1, R), F32), V((Z, 1, R), F32),
        V((NC, X, Q, 2 * R), F32), V((NC, 2, HQ, 2 * R), BF16), V((NC, 2, HQ, 2 * R), BF16),
        V((NC, 2, HQ, 2 * R), BF16), V((NC, 2, HQ, 2 * R), BF16), V((NC, 2, HQ, 2 * R), F32), V((NC, 2, HQ, 2 * R), F32),
        V((NC, 2, Q, R), F32), V((Z, Q, R), F32), V((NC, 2, Q, R), BF16), V((Z, Q, R), BF16), V((X, Q, R), F32),
        V((Y, T, D), F32), V((Y, T, D), F32), V((2, HT, D), BF16), V((2, HT, D), BF16), V((4, HT, D), F32),
        V((2, 2, HT, D), BF16), V((2, 2, HT, D), BF16), V((R, D), F32),
        dma((Z,)), dma((3,)), pltpu.SemaphoreType.REGULAR, dma((GROUPS,)), dma((5,)), dma((5,)), *[dma((1,))] * 7,
        dma((NC,)), dma((NC,)), dma((NC,)), dma((1,)), dma((1,)), dma((1,)), dma((Y,)), dma((1,)), dma((1,)),
    ]
    out = pl.pallas_call(
        functools.partial(kernel, X, Z),
        out_shape=pltpu.VMEM((T + R, D), F32),
        in_specs=[hbm, hbm, hbm],
        out_specs=pl.BlockSpec(memory_space=pltpu.VMEM),
        scratch_shapes=scratch,
        compiler_params=pltpu.CompilerParams(
            collective_id=0, has_side_effects=True, vmem_limit_bytes=56 << 20
        ),
        name="head",
    )(prototypes, teacher_embed, student_embed)
    return pl.pallas_call(
        split,
        out_shape=(jax.ShapeDtypeStruct((T, D), F32), jax.ShapeDtypeStruct((R, D), F32)),
        in_specs=[pl.BlockSpec(memory_space=pltpu.VMEM)],
        out_specs=(hbm, hbm),
        scratch_shapes=[dma((2,))],
        name="split",
    )(pltpu.with_memory_space_constraint(out, pltpu.VMEM))


def solution(mesh):
    X = mesh.shape["proto"]
    Z = mesh.shape["batch"] // (Y * C)
    placed = (P("proto", None), P("batch", None), P("batch", None))
    return jax.shard_map(
        functools.partial(local, X, Z),
        mesh=mesh,
        in_specs=placed,
        out_specs=(P(("proto", "batch"), None), P("batch", None)),
        check_vma=False,
    )
```

```python
import functools
import math

import jax
import jax.numpy as jnp
from jax import lax
from jax.experimental import pallas as pl
from jax.experimental.pallas import tpu as pltpu
from jax.sharding import PartitionSpec as P

Y = 4
C = 2
LOG2E = 1.4426950408889634
TEACHER = LOG2E / 0.07
STUDENT = LOG2E / 0.1
LANES = 128
MESH = pl.DeviceIdType.MESH
NT = (((1,), (1,)), ((), ()))
F32 = jnp.float32
BF16 = jnp.bfloat16
GROUPS = 5
NARROW = (1, 2)


def dot_nt(a, b):
    return lax.dot_general(a, b, NT, preferred_element_type=F32)


def dot(a, b):
    return jnp.dot(a, b, preferred_element_type=F32)


def kernel(
    X, Z, p_hbm, te_hbm, se_hbm, out_hbm,
    p_v, te_all, se_all, ss, init, pe, sg, pt,
    tmx, tmx_r, pk_all, sst, sst_r, sg_all,
    csp, cs, cs_r, csc, rt, rt_r, rz, rz_r, af, bf,
    gacc, hx_s, hx_r, gsx_s, gsx_r, gxs_s, gxs_r, gsz_s, gsz_r, gszb_s, gszb_r, gsf,
    gpc_s, gpc_r, hy_s, hy_r, gy, gpy_s, gpy_r, gs_v,
    p_sem, o_sem, in_sem, out_sem, te_rs, se_rs, tx_rs, tz_rs, sx_rs, sz_rs, cs_rs, rx_rs, rz_rs,
    hx_rs, gx_rs, gxs_rs, gz_rs, gzb_rs, gf_rs, pc_rs, hy_rs, py_rs,
):
    b = lax.axis_index("batch")
    x = lax.axis_index("proto")
    z = b // (Y * C)
    y = (b // C) % Y
    c = b % C
    NP, D = p_v.shape
    KB = NP // Z
    T = KB // (Y * C)
    R = te_all.shape[1]
    NC = Z // 2
    NT8 = KB // T

    def dev(x_, z_, y_, c_):
        return {"batch": (z_ * Y + y_) * C + c_, "proto": x_}

    xs = [dev((x + d) % X, z, y, c) for d in range(X)]
    zs = [dev(x, (z + d) % Z, y, c) for d in range(Z)]
    far_x = sorted(range(1, X), key=lambda d: -min(d, X - d))
    far_z = sorted(range(1, Z), key=lambda d: -min(d, Z - d))
    far_yc = sorted(range(1, Y * C), key=lambda i: -min(i % Y, Y - i % Y))
    ycs = [(dy, dc) for dc in range(C) for dy in range(Y)]
    yc = [dev(x, z, (y + dy) % Y, (c + dc) % C) for dy, dc in ycs]
    sent = [0] * GROUPS

    def send(src, dst, rsem, to, group):
        pltpu.make_async_remote_copy(
            src_ref=src, dst_ref=dst, send_sem=out_sem.at[group], recv_sem=rsem, device_id=to, device_id_type=MESH
        ).start()
        sent[group] += math.prod(src.shape) * src.dtype.itemsize

    def arrived(dst, rsem):
        pltpu.make_async_remote_copy(
            src_ref=dst, dst_ref=dst, send_sem=out_sem.at[0], recv_sem=rsem, device_id=xs[1], device_id_type=MESH
        ).wait_recv()

    own_t = pltpu.make_async_copy(te_hbm, te_all.at[z], o_sem.at[0])
    own_s = pltpu.make_async_copy(se_hbm, se_all.at[z], o_sem.at[1])
    own_t.start()
    own_s.start()

    def load(i):
        at = pl.multiple_of(i * KB, KB)
        return pltpu.make_async_copy(p_hbm.at[pl.ds(at, KB)], p_v.at[pl.ds(at, KB)], p_sem.at[i])

    ahead = min(4, Z)
    for i in range(2):
        load(i).start()
    barrier = pltpu.get_barrier_semaphore()
    near = (1, 2, 6, 7) if Z == 8 else range(1, Z)
    peers = xs[1:] + [zs[d] for d in near] + yc[1:]
    for peer in peers:
        pl.semaphore_signal(barrier, inc=1, device_id=peer, device_id_type=MESH)
    own_t.wait()
    own_s.wait()
    for i in range(2, ahead):
        load(i).start()

    HR = R // 2

    def gather_near(full, rs, group):
        if Z != 8:
            for d in range(1, Z):
                send(full.at[z], full.at[z], rs.at[4], zs[d], group)
            return
        for part in range(2):
            for d in (2, 6):
                low_half = (part == 0) == (d == 2)
                rows = pl.ds(0 if low_half else HR, HR)
                send(full.at[z, rows], full.at[z, rows], rs.at[part + (0 if d == 2 else 2)], zs[d], group)
        for d in (1, 7):
            send(full.at[z], full.at[z], rs.at[5], zs[d], group)

    def gather_far(full, rs, group):
        if Z != 8:
            return
        for part in range(2):
            for d in (2, 6):
                src = lax.rem(z + 8 - d, 8)
                low_half = (part == 0) == (d == 2)
                rows = pl.ds(0 if low_half else HR, HR)
                arrived(full.at[src, rows], rs.at[part + (0 if d == 2 else 2)])
                if part == 0:
                    send(full.at[src, rows], full.at[src, rows], rs.at[4], zs[d], group)
                send(full.at[src, rows], full.at[src, rows], rs.at[4], zs[1 if d == 2 else 7], group)

    def gather_one(full, rs):
        if Z == 8:
            arrived(full.at[pl.ds(0, 2)], rs.at[5])

    def gather_end(full, rs):
        arrived(full.at[pl.ds(0, 3 if Z == 8 else Z - 1)], rs.at[4])

    own = jnp.concatenate([te_all[z], se_all[z]], axis=0)
    low = jnp.full((32, R), -jnp.inf, F32)

    def stats(i, carry, n=1):
        tm, sm = carry
        for k in range(n):
            load(i + k).wait()
        for k in range(n):

            @pl.when(i + k + ahead < Z)
            def _():
                load(i + k + ahead).start()

        at = pl.multiple_of(i * KB, KB)
        s = dot_nt(p_v[pl.ds(at, n * KB), :], own)
        ts = s[:, :R]
        st = s[:, R:]
        ss[pl.ds(at, n * KB), :] = st
        tm = jnp.maximum(tm, jnp.max(ts.reshape(n * KB // 32, 32, R), axis=0))
        sm = jnp.maximum(sm, jnp.max(st.reshape(n * KB // 32, 32, R), axis=0))
        return tm, sm

    def stats_pair(k, tops):
        return stats(2 * k, tops, 2)

    early = 1
    tops = lax.fori_loop(0, early, stats_pair, (low, low))
    pl.semaphore_wait(barrier, len(peers))
    if Z == 8:
        for d in (2, 6):
            pl.semaphore_signal(in_sem, inc=1, device_id=zs[d], device_id_type=MESH)
    gather_near(te_all, te_rs, 0)
    tops = lax.fori_loop(early, NC, stats_pair, tops)
    tmx[...] = jnp.max(tops[0], axis=0, keepdims=True) * TEACHER
    for d in far_x:
        send(tmx, tmx_r.at[d], tx_rs.at[0], xs[d], 4)

    s_top = jnp.max(tops[1], axis=0, keepdims=True) * STUDENT
    step = min(512, KB)

    def mass(k, acc):
        at = pl.multiple_of(k * step, step)
        e = jnp.exp2(ss[pl.ds(at, step), :] * STUDENT - s_top)
        return acc + jnp.sum(e.reshape(step // 32, 32, R), axis=0)

    half = NP // step // 2
    acc = lax.fori_loop(0, half, mass, jnp.zeros((32, R), F32))
    peak = tmx[...]
    arrived(tmx_r.at[pl.ds(1, X - 1)], tx_rs.at[0])
    for d in range(1, X):
        peak = jnp.maximum(peak, tmx_r[d])
    if Z == 8:
        pl.semaphore_wait(in_sem, 2)
    pk_all[z] = peak
    for d in far_z:
        send(pk_all.at[z], pk_all.at[z], tz_rs.at[0 if d in near else 1], zs[d], 4)
    gather_far(te_all, te_rs, 0)
    acc = lax.fori_loop(half, NP // step, mass, acc)
    sst[0] = s_top
    sst[1] = jnp.sum(acc, axis=0, keepdims=True)
    for d in range(1, X):
        send(sst, sst_r.at[d], sx_rs.at[0], xs[d], 4)
    for k in range(NT8):
        tile = p_v[pl.ds(pl.multiple_of(z * KB + k * T, T), T), :]
        pt[:, k * T : (k + 1) * T] = tile.T
    def pair(ref, j):
        return jnp.concatenate([ref[2 * j], ref[2 * j + 1]], axis=0)

    def row_pair(ref, j):
        return jnp.concatenate([ref[2 * j], ref[2 * j + 1]], axis=1)

    block = p_v.at[pl.ds(pl.multiple_of(z * KB, KB), KB)]
    def teach(o, first=False):
        j = lax.rem(z // 2 + o, NC)
        e = jnp.exp2(dot_nt(block[...], pair(te_all, j)) * TEACHER - row_pair(pk_all, j))
        init[j] = e
        e = e[:, :R] + e[:, R:]
        csp[...] = e if first else csp[...] + e

    if Z == 8:
        gather_one(te_all, te_rs)
        arrived(pk_all.at[pl.ds(0, 4)], tz_rs.at[0])
        teach(0, True)
        teach(3 - 2 * (z % 2))
        arrived(pk_all.at[pl.ds(0, 3)], tz_rs.at[1])
        gather_end(te_all, te_rs)
        gather_near(se_all, se_rs, 1)
        teach(1 + 2 * (z % 2))
        teach(2)
    else:
        arrived(pk_all.at[pl.ds(0, Z - 1)], tz_rs.at[0])
        gather_end(te_all, te_rs)
        gather_near(se_all, se_rs, 1)
        for o in range(NC):
            teach(o, o == 0)
    for h in range(KB // LANES):
        cs[h] = jnp.sum(csp[h * LANES : (h + 1) * LANES].T, axis=0, keepdims=True)
    for i in far_yc:
        send(cs, cs_r.at[i], cs_rs.at[0], yc[i], 0)
    arrived(sst_r.at[pl.ds(1, X - 1)], sx_rs.at[0])
    top = sst[0]
    for d in range(1, X):
        top = jnp.maximum(top, sst_r[d, 0])
    total = sst[1] * jnp.exp2(sst[0] - top)
    for d in range(1, X):
        total = total + sst_r[d, 1] * jnp.exp2(sst_r[d, 0] - top)
    sg_all[z, 0] = top
    sg_all[z, 1] = total
    for d in range(1, Z):
        send(sg_all.at[z], sg_all.at[z], sz_rs.at[0], zs[d], 4)
    tot = cs[...]
    arrived(cs_r.at[pl.ds(1, Y * C - 1)], cs_rs.at[0])
    for i in range(1, Y * C):
        tot = tot + cs_r[i]
    csc[...] = 1.0 / tot

    def rows(k, accs):
        at = pl.multiple_of(k * LANES, LANES)
        scale = jnp.broadcast_to(csc[k], (LANES, LANES)).T
        out = []
        for j in range(NC):
            for h in range(2):
                v = init[j, pl.ds(at, LANES), h * R : (h + 1) * R] * scale
                init[j, pl.ds(at, LANES), h * R : (h + 1) * R] = v
                out.append(accs[2 * j + h] + jnp.sum(v.reshape(LANES // 8, 8, R), axis=0))
        return tuple(out)

    accs = lax.fori_loop(0, KB // LANES, rows, tuple(jnp.zeros((8, R), F32) for _ in range(Z)), unroll=16)
    for i in range(Z):
        rt[i] = jnp.sum(accs[i], axis=0, keepdims=True)
    for d in far_x:
        send(rt, rt_r.at[d], rx_rs.at[0], xs[d], 0)
    gather_far(se_all, se_rs, 1)

    def learn(j):
        tops_j = jnp.concatenate([sg_all[2 * j, 0], sg_all[2 * j + 1, 0]], axis=1)
        pe[j] = jnp.exp2(dot_nt(block[...], pair(se_all, j)) * STUDENT - tops_j) * row_pair(af, j)

    tot = rt[...]
    arrived(rt_r.at[pl.ds(1, X - 1)], rx_rs.at[0])
    for d in range(1, X):
        tot = tot + rt_r[d]
    rz[...] = tot
    for d in far_z:
        send(rz, rz_r.at[d], rz_rs.at[0], zs[d], 0)
    gather_one(se_all, se_rs)
    gather_end(se_all, se_rs)
    arrived(sg_all.at[pl.ds(0, Z - 1)], sz_rs.at[0])
    for i in range(Z):
        af[i] = 10.0 / sg_all[i, 1]
    for j in range(NC):
        learn(j)
    tot = rz[...]
    arrived(rz_r.at[pl.ds(1, Z - 1)], rz_rs.at[0])
    for d in range(1, Z):
        tot = tot + rz_r[d]
    bf[...] = 10.0 / tot

    Q = D // X
    HQ = Q // 2
    HT = T // 2
    narrow = NARROW if NC == 4 else ()
    order = [2, 1, 3, 0] if NC == 4 else list(range(1, NC)) + [0]

    def piece(o, d):
        return gacc.at[o, lax.rem(x + d, X)]

    def x_relayed(o):
        for side in range(2):
            to = xs[1 if side == 0 else 3]
            hx_s[o, side] = piece(o, 2)[side * HQ : (side + 1) * HQ].astype(BF16)
            send(hx_s.at[o, side], hx_r.at[o, side], hx_rs.at[o], to, 2)

    def x_direct(o):
        for side in range(2):
            to = xs[1 if side == 0 else 3]
            at = (1 - side) * HQ
            gsx_s[o, side] = piece(o, 1 if side == 0 else 3)[at : at + HQ].astype(BF16)
            send(gsx_s.at[o, side], gsx_r.at[o, side], gx_rs.at[o], to, 2)

    def x_second(o):
        arrived(hx_r.at[o], hx_rs.at[o])
        for side in range(2):
            at = side * HQ
            gxs_s[o, side] = piece(o, 1 if side == 0 else 3)[at : at + HQ] + hx_r[o, side].astype(F32)
            send(gxs_s.at[o, side], gxs_r.at[o, side], gxs_rs.at[o], xs[1 if side == 0 else 3], 2)

    def x_third(o):
        j = lax.rem(z // 2 + o, NC)
        arrived(gsx_r.at[o], gx_rs.at[o])
        arrived(gxs_r.at[o], gxs_rs.at[o])
        keep, there, rsem = (gszb_s, gszb_r, gzb_rs) if o in narrow else (gsz_s, gsz_r, gz_rs)
        for part in range(2):
            at = part * HQ
            tot = piece(o, 0)[at : at + HQ] + gxs_r[o, part] + gsx_r[o, 1 - part].astype(F32)
            for h in range(2):
                keep[o, h, at : at + HQ] = tot[:, h * R : (h + 1) * R].astype(keep.dtype)
        for h in range(1 if o == 0 else 2):
            to = 1 - z % 2 if o == 0 else h
            send(keep.at[o, to], there.at[z], rsem.at[0], dev(x, 2 * j + to, y, c), 2)

    for n in range(0, NC, 2):
        group = order[n : n + 2]
        gs = []
        for o in group:
            j = lax.rem(z // 2 + o, NC)
            g = (pe[j] - init[j] * row_pair(bf, j)).astype(BF16)
            sg[j] = g
            gs.append(g)
        acc = dot(pt[...], jnp.concatenate(gs, axis=1))
        for i, o in enumerate(group):
            for q in range(X):
                gacc[o, q] = acc[q * Q : (q + 1) * Q, i * 2 * R : (i + 1) * 2 * R]
            x_relayed(o)

    for o in order:
        x_direct(o)

    def proto_tiles(deltas, c_):
        lhs = []
        for d in deltas:
            at = pl.multiple_of((lax.rem(y + d, Y) * C + c_) * T, T)
            lhs.append(jnp.concatenate([sg[j, pl.ds(at, T), :] for j in range(NC)], axis=1))
        return dot(jnp.concatenate(lhs, axis=0), se_all[...].reshape(Z * R, D))

    partner = yc[Y]

    def to_partner(n, deltas):
        g = proto_tiles(deltas, 1 - c)
        for i in range(len(deltas)):
            gpc_s[n + i] = g[i * T : (i + 1) * T]
        send(gpc_s.at[pl.ds(n, len(deltas))], gpc_r.at[pl.ds(n, len(deltas))], pc_rs.at[n], partner, 3)

    def to_y(side, part, value):
        gpy_s[side, part] = value.astype(BF16)
        send(gpy_s.at[side, part], gpy_r.at[side, part], py_rs.at[0], yc[1 if side == 0 else 3], 3)

    steps = [("s", o) for o in order] + [("t", o) for o in order]

    def advance(count):
        for _ in range(min(count, len(steps))):
            kind, o = steps.pop(0)
            (x_second if kind == "s" else x_third)(o)

    to_partner(0, (2,))
    to_partner(1, (1, 3))
    advance(1)
    g = proto_tiles((2,), c)
    advance(3)
    arrived(gpc_r.at[pl.ds(0, 1)], pc_rs.at[0])
    for side in range(2):
        at = side * HT
        hy_s[side] = (g[at : at + HT] + gpc_r[0, at : at + HT]).astype(BF16)
        send(hy_s.at[side], hy_r.at[side], hy_rs.at[0], yc[1 if side == 0 else 3], 3)
    to_partner(3, (0,))
    g = proto_tiles((1, 3), c)
    advance(2)
    arrived(gpc_r.at[pl.ds(1, 2)], pc_rs.at[1])
    to_y(0, 1, g[HT:T] + gpc_r[1, HT:])
    gy[0] = g[:HT] + gpc_r[1, :HT]
    to_y(1, 0, g[T : T + HT] + gpc_r[2, :HT])
    gy[1] = g[T + HT :] + gpc_r[2, HT:]
    advance(len(steps))
    g = proto_tiles((0,), c)
    gy[2] = g[:HT]
    gy[3] = g[HT:]
    arrived(hy_r, hy_rs.at[0])
    to_y(0, 0, gy[0] + hy_r[0].astype(F32))
    to_y(1, 1, gy[1] + hy_r[1].astype(F32))
    arrived(gsz_r.at[pl.ds(0, Z - 1 - 2 * len(narrow))], gz_rs.at[0])
    if narrow:
        arrived(gszb_r.at[pl.ds(0, 2 * len(narrow))], gzb_rs.at[0])
    tot = gsz_s[0, z % 2]
    tot = tot + gsz_r[z + 1 - 2 * (z % 2)]
    for o in range(1, NC):
        j = lax.rem(z // 2 + o, NC)
        for h in range(2):
            tot = tot + (gszb_r if NC - o in narrow else gsz_r)[2 * j + h].astype(F32)
    gsf[x] = tot
    for d in far_x:
        send(gsf.at[x], gsf.at[x], gf_rs.at[0], xs[d], 3)
    arrived(gpy_r, py_rs.at[0])
    arrived(gpc_r.at[pl.ds(3, 1)], pc_rs.at[3])
    for part in range(2):
        tot = gy[2 + part] + gpc_r[3, part * HT : (part + 1) * HT]
        for side in range(2):
            tot = tot + gpy_r[side, part].astype(F32)
        out_hbm[pl.ds(part * HT, HT), :] = tot
    arrived(gsf.at[pl.ds(0, X - 1)], gf_rs.at[0])
    full = gsf[...].reshape(D, R)
    for h in range(D // LANES):
        out_hbm[pl.ds(T, R), h * LANES : (h + 1) * LANES] = full[h * LANES : (h + 1) * LANES].T
    for group, size in enumerate(sent):
        n = size // (2 * D)
        whole = cs_r.at[pl.ds(0, 2), pl.ds(0, n // 2)] if group == 4 else p_v.at[pl.ds(0, n)]
        pltpu.make_async_remote_copy(
            src_ref=whole, dst_ref=whole, send_sem=out_sem.at[group],
            recv_sem=tx_rs.at[0], device_id=xs[1], device_id_type=MESH,
        ).wait_send()


def split(in_v, gp_hbm, gs_hbm, o_sem):
    T = gp_hbm.shape[0]
    R = gs_hbm.shape[0]
    outs = [
        pltpu.make_async_copy(in_v.at[pl.ds(0, T)], gp_hbm, o_sem.at[0]),
        pltpu.make_async_copy(in_v.at[pl.ds(T, R)], gs_hbm, o_sem.at[1]),
    ]
    for out in outs:
        out.start()
    for out in outs:
        out.wait()


def local(X, Z, prototypes, teacher_embed, student_embed):
    NP, D = prototypes.shape
    R = teacher_embed.shape[0]
    KB = NP // Z
    T = KB // (Y * C)
    NC = Z // 2
    Q = D // X
    HQ = Q // 2
    HT = T // 2
    V = pltpu.VMEM
    dma = pltpu.SemaphoreType.DMA
    hbm = pl.BlockSpec(memory_space=pl.ANY)
    scratch = [
        V((NP, D), BF16), V((Z, R, D), BF16), V((Z, R, D), BF16), V((NP, R), F32),
        V((NC, KB, 2 * R), F32), V((NC, KB, 2 * R), F32), V((NC, KB, 2 * R), BF16), V((D, KB), BF16),
        V((1, R), F32), V((X, 1, R), F32), V((Z, 1, R), F32),
        V((2, 1, R), F32), V((X, 2, 1, R), F32), V((Z, 2, 1, R), F32),
        V((KB, R), F32), V((KB // LANES, 1, LANES), F32), V((Y * C, KB // LANES, 1, LANES), F32),
        V((KB // LANES, 1, LANES), F32),
        V((Z, 1, R), F32), V((X, Z, 1, R), F32), V((Z, 1, R), F32), V((Z, Z, 1, R), F32),
        V((Z, 1, R), F32), V((Z, 1, R), F32),
        V((NC, X, Q, 2 * R), F32), V((NC, 2, HQ, 2 * R), BF16), V((NC, 2, HQ, 2 * R), BF16),
        V((NC, 2, HQ, 2 * R), BF16), V((NC, 2, HQ, 2 * R), BF16), V((NC, 2, HQ, 2 * R), F32), V((NC, 2, HQ, 2 * R), F32),
        V((NC, 2, Q, R), F32), V((Z, Q, R), F32), V((NC, 2, Q, R), BF16), V((Z, Q, R), BF16), V((X, Q, R), F32),
        V((Y, T, D), F32), V((Y, T, D), F32), V((2, HT, D), BF16), V((2, HT, D), BF16), V((4, HT, D), F32),
        V((2, 2, HT, D), BF16), V((2, 2, HT, D), BF16), V((R, D), F32),
        dma((Z,)), dma((3,)), pltpu.SemaphoreType.REGULAR, dma((GROUPS,)), dma((6,)), dma((6,)), dma((1,)), dma((2,)), *[dma((1,))] * 5,
        dma((NC,)), dma((NC,)), dma((NC,)), dma((1,)), dma((1,)), dma((1,)), dma((Y,)), dma((1,)), dma((1,)),
    ]
    out = pl.pallas_call(
        functools.partial(kernel, X, Z),
        out_shape=pltpu.VMEM((T + R, D), F32),
        in_specs=[hbm, hbm, hbm],
        out_specs=pl.BlockSpec(memory_space=pltpu.VMEM),
        scratch_shapes=scratch,
        compiler_params=pltpu.CompilerParams(
            collective_id=0, has_side_effects=True, vmem_limit_bytes=56 << 20
        ),
        name="head",
    )(prototypes, teacher_embed, student_embed)
    return pl.pallas_call(
        split,
        out_shape=(jax.ShapeDtypeStruct((T, D), F32), jax.ShapeDtypeStruct((R, D), F32)),
        in_specs=[pl.BlockSpec(memory_space=pltpu.VMEM)],
        out_specs=(hbm, hbm),
        scratch_shapes=[dma((2,))],
        name="split",
    )(pltpu.with_memory_space_constraint(out, pltpu.VMEM))


def solution(mesh):
    X = mesh.shape["proto"]
    Z = mesh.shape["batch"] // (Y * C)
    placed = (P("proto", None), P("batch", None), P("batch", None))
    return jax.shard_map(
        functools.partial(local, X, Z),
        mesh=mesh,
        in_specs=placed,
        out_specs=(P(("proto", "batch"), None), P("batch", None)),
        check_vma=False,
    )
```
